256 devices in a mesh: pix: 64 (over y, z, core), plane: 4 (over x).
Axes of the slice: x: 4, y: 4, z: 8, core: 2. Of those that a mesh axis runs over, the one named last changes fastest.
Arguments:
- movie: bfloat16 [4, 2048, 256, 256], P('plane', 'pix'), may hold values from -6 to 6
- footprints: bfloat16 [4, 8192, 1024], P('plane', 'pix'), may hold values from 0 to 0.019897461
- traces: bfloat16 [4, 8192, 256], P('plane', 'pix'), may hold values from 0 to 2
- stripe: int32 [4, 8192, 1], P('plane', 'pix'), may hold values from 0 to 63; in each aligned block of 128 rows (0 to 127, 128 to 255, ..., all dimensions but the last counted through in order) at most 4 rows name the same one
- column: int32 [4, 8192], P('plane', 'pix'), may hold values from 0 to 224
- annulus_gain: float32 [4, 256], P('plane'), may hold values from 1 to 8
- decay_slow: float32 [4, 8192], P('plane', 'pix'), may hold values from 0.4 to 0.9
- decay_fast: float32 [4, 8192], P('plane', 'pix'), may hold values from 0.05 to 0.3
Outputs:
- background: bfloat16 [4, 2048, 256, 256], P('plane', 'pix')
- traces_new: float32 [4, 8192, 256], P('plane', 'pix')
The draws below stay inside these ranges and needn't reach their ends.
Inputs may be any that keep to these rules, and one draw needn't show every extreme that they name: Among the 128 neurons of one device (aligned blocks of 128 neurons of a plane), no stripe is named more than 4 times, and some device names one stripe exactly 4 times.
All inputs are finite; a program needn't handle non-finite values.
Results may differ from the reference program's by a relative error of at most 0.001.
The reference program's roundings to bfloat16 on the way count: a program that leaves them out, or rounds other values in their place, can miss the bound.
Values may be sent and summed in bfloat16 or wider, within the bound.
A program may use at most 128 MiB of HBM per device.

```python
import math
import jax
import jax.numpy as jnp
import numpy as np
from jax import lax

FOOT = 32
RAD = 12
GR = 3
COLS = 256
FRAMES = 256
NEUR_DEV = 128
PLANES = 4
HEIGHT = 2048
NEUR = 8192
CAP = 4
N_PIX = 64


def touch_ends(drawn, stream_key, smallest, largest):
    shape = drawn.shape
    spot = [jax.random.randint(jax.random.fold_in(stream_key, axis), (), 0, shape[axis]) for axis in range(len(shape))]
    drawn = drawn.at[tuple(spot)].set(smallest)
    longest = shape.index(max(shape))
    spot[longest] = (spot[longest] + 1) % shape[longest]
    return drawn.at[tuple(spot)].set(largest)


def levels(key, extent, shards, low, top_value):
    loudness, own = 1.0, jax.random.fold_in(key, 6)
    for position, parts in shards:
        draws = jnp.exp(jax.random.uniform(jax.random.fold_in(own, position), (parts,), jnp.float32, low / len(shards), top_value / len(shards)))
        loudness = loudness * jnp.repeat(draws, extent[position] // parts).reshape([-1 if axis == position else 1 for axis in range(len(extent))])
    return loudness


def deal_out(key, own, number, rows, amount, top, most, skew):
    ranking = jax.random.permutation(key, amount)
    packed, ordinary = load_shares(amount, rows * top, most, skew, True), load_shares(amount, rows * top, most, skew, False)
    places = jnp.arange(amount)

    def named(tallies, turn):
        used = int((tallies > 0).sum())
        fixed = max(1, used // 4)
        moved = fixed + (places - fixed + turn * (used - fixed)) % max(1, amount - fixed)
        return jnp.zeros((amount,), jnp.int32).at[ranking[jnp.where(places < fixed, places, moved)]].set(jnp.asarray(tallies, jnp.int32))

    tallies = jnp.where(number % 4 == 0, named(packed, number // 4), named(ordinary, number - number // 4 - 1))
    mixed = jax.random.permutation(jax.random.fold_in(own, 3), amount)
    donor, sink = mixed[0:amount // 2 * 2:2], mixed[1:amount // 2 * 2:2]
    room = jnp.minimum(tallies[donor] - 1, most - tallies[sink]) // 2
    room = jnp.where((donor == ranking[0]) | (sink == ranking[0]) | (tallies[sink] == 0), 0, jnp.maximum(room, 0))
    moved = jax.random.randint(jax.random.fold_in(own, 4), (amount // 2,), 0, 1 << 20) % (room + 1)
    tallies = tallies.at[donor].add(-moved).at[sink].add(moved)
    members = jnp.searchsorted(jnp.cumsum(tallies), jnp.arange(rows * top), side="right").astype(jnp.int32)
    listing = members.reshape(top, rows).T
    listing = listing[jax.random.permutation(jax.random.fold_in(own, 1), rows)]
    turn = jax.random.randint(jax.random.fold_in(own, 2), (rows, 1), 0, top)
    return jnp.take_along_axis(listing, (jnp.arange(top)[None, :] + turn) % top, axis=1)


def load_shares(amount, total, reach, skew, full):
    loads = [(1 << 20) // math.isqrt(rank ** skew) + 1 for rank in range(1, amount + 1)]
    largest = reach if full else min(reach, max(-(-total // amount), total * loads[0] // sum(loads)))
    least = 1 if total - largest >= amount - 1 else 0
    holding, rest = [largest] + [least] * (amount - 1), total - largest - least * (amount - 1)
    while rest > 0:
        candidates = [i for i in range(1, amount) if holding[i] < largest] or [i for i in range(1, amount) if holding[i] < reach]
        whole, left = sum([loads[i] for i in candidates]), rest
        for i in candidates:
            more = min(reach - holding[i], max(1, left * loads[i] // whole), rest)
            holding[i] = holding[i] + more
            rest = rest - more
    return np.array(holding)


def normal_values(rng, shape, width, most, cuts=(), dtype=jnp.bfloat16):
    result = jax.random.normal(rng, shape, jnp.float32) * width
    if len(cuts) > 0:
        result = levels(rng, shape, cuts, -0.22, 0.18) * result
    return jnp.clip(result, min=-most, max=most).astype(dtype)


def setup_inputs(seed: int = 0) -> dict:
    seeds = jax.random.split(jax.random.key(seed), 9)
    movie = normal_values(seeds[0], (PLANES, HEIGHT, COLS, FRAMES), 1.0, 6.0, ((0, 4), (1, 64)))
    footprints = jnp.clip(0.019897461 * jax.random.uniform(seeds[1], (PLANES, NEUR, FOOT * FOOT), jnp.float32) ** levels(seeds[1], (PLANES, NEUR, FOOT * FOOT), ((0, 4), (1, 64)), -0.2, 0.2), 0.0, 0.019897461).astype(jnp.bfloat16)
    traces = jnp.clip(2.0 * jax.random.uniform(seeds[2], (PLANES, NEUR, FRAMES), jnp.float32) ** levels(seeds[2], (PLANES, NEUR, FRAMES), ((0, 4), (1, 64)), -0.2, 0.2), 0.0, 2.0).astype(jnp.bfloat16)
    stripe_keys = jax.random.split(jax.random.fold_in(seeds[3], 1), PLANES * NEUR // NEUR_DEV)
    stripe_turns = jax.random.permutation(jax.random.fold_in(seeds[3], 3), PLANES * NEUR // NEUR_DEV)
    stripe = jax.vmap(lambda own, number: deal_out(jax.random.fold_in(seeds[3], 2), own, number, NEUR_DEV, N_PIX, 1, CAP, 2))(stripe_keys, stripe_turns).reshape((PLANES, NEUR, 1))
    column = touch_ends(jax.random.randint(seeds[4], (PLANES, NEUR), 0, COLS - FOOT + 1), jax.random.fold_in(seeds[4], 1), 0, COLS - FOOT).astype(jnp.int32)
    annulus_gain = jnp.clip(jnp.exp(math.log(8.0) - 2.0794415 * jax.random.uniform(seeds[5], (PLANES, COLS), jnp.float32) ** levels(seeds[5], (PLANES, COLS), ((0, 4),), -0.2, 0.2)), 1.0, 8.0)
    decay_slow = jnp.clip(jnp.exp(math.log(0.9) - 0.8109302 * jax.random.uniform(seeds[6], (PLANES, NEUR), jnp.float32) ** levels(seeds[6], (PLANES, NEUR), ((0, 4), (1, 64)), -0.2, 0.2)), 0.4, 0.9)
    decay_fast = jnp.clip(jnp.exp(math.log(0.3) - 1.7917595 * jax.random.uniform(seeds[7], (PLANES, NEUR), jnp.float32) ** levels(seeds[7], (PLANES, NEUR), ((0, 4), (1, 64)), -0.2, 0.2)), 0.05, 0.3)
    return dict(movie=movie, footprints=footprints, traces=traces, stripe=stripe, column=column, annulus_gain=annulus_gain, decay_slow=decay_slow, decay_fast=decay_fast)


lam_floor = 0.1
noise_eps = 1e-05
norm_eps = 1e-05
sigma_twice = 4.5

def kernel_taps(radius):
    offsets = jnp.arange(-radius, radius + 1).astype(jnp.float32)
    shape_raw = jnp.exp(-offsets * offsets / sigma_twice)
    return (shape_raw / jnp.sum(shape_raw)).astype(jnp.bfloat16)

def deconvolve(updated, decay_slow, decay_fast):
    lag_one = jnp.pad(updated, ((0, 0), (1, 0)))[:, :-1]
    lag_two = jnp.pad(updated, ((0, 0), (2, 0)))[:, :-2]
    driven = updated - (decay_slow + decay_fast)[:, None] * lag_one + (decay_slow * decay_fast)[:, None] * lag_two
    return jnp.maximum(driven - lam_floor, 0.0)

def reconvolve(spikes, decay_slow, decay_fast):
    frame_count = spikes.shape[1]
    frame_index = jnp.arange(frame_count)
    frame_lag = frame_index[:, None] - frame_index[None, :]
    exponent = (jnp.maximum(frame_lag, 0) + 1).astype(jnp.float32)
    kernel_rise = jnp.exp(exponent[None] * jnp.log(decay_slow)[:, None, None]) - jnp.exp(exponent[None] * jnp.log(decay_fast)[:, None, None])
    kernel_scale = (1.0 - decay_slow) * (1.0 - decay_fast) / (decay_slow - decay_fast)
    kernel = jnp.where(frame_lag[None] >= 0, kernel_rise * kernel_scale[:, None, None], 0.0)
    return jnp.einsum('ntk,nk->nt', kernel, spikes, precision=lax.Precision.HIGHEST)

def box_sum(field_values, half_width, along_axis):
    length_along = field_values.shape[along_axis]
    pad_spec = [(0, 0)] * field_values.ndim
    pad_spec[along_axis] = (half_width + 1, half_width)
    running = jnp.cumsum(jnp.pad(field_values, pad_spec), axis=along_axis)
    upper_part = lax.slice_in_dim(running, 2 * half_width + 1, 2 * half_width + 1 + length_along, axis=along_axis)
    lower_part = lax.slice_in_dim(running, 0, length_along, axis=along_axis)
    return upper_part - lower_part

def blur_along(field_values, weights, along_axis):
    length_along = field_values.shape[along_axis]
    pad_spec = [(0, 0)] * field_values.ndim
    pad_spec[along_axis] = (GR, GR)
    padded_values = jnp.pad(field_values, pad_spec)
    running_total = jnp.zeros_like(field_values)
    for offset in range(2 * GR + 1):
        running_total = running_total + weights[offset] * lax.slice_in_dim(padded_values, offset, offset + length_along, axis=along_axis)
    return running_total

def reference(movie, footprints, traces, stripe, column, annulus_gain, decay_slow, decay_fast):
    height = movie.shape[1]
    col_count = movie.shape[2]
    frame_count = movie.shape[3]
    weights = kernel_taps(GR).astype(jnp.float32)
    backgrounds = []
    detrended_list = []
    noise_list = []
    for plane_index in range(PLANES):

        def add_tile(model_image, item_parts):
            tile_values, trace_values, stripe_value, column_value = item_parts
            patch = tile_values.astype(jnp.float32).reshape(FOOT, FOOT)[:, :, None] * trace_values.astype(jnp.float32)[None, None, :]
            start = ((stripe_value * FOOT).astype(jnp.int32), column_value.astype(jnp.int32), jnp.int32(0))
            current = lax.dynamic_slice(model_image, start, (FOOT, FOOT, frame_count))
            return (lax.dynamic_update_slice(model_image, current + patch, start), None)
        model_image, _ = lax.scan(add_tile, jnp.zeros((height, col_count, frame_count), jnp.float32), (footprints[plane_index], traces[plane_index], stripe[plane_index, :, 0], column[plane_index]))
        residual = (movie[plane_index].astype(jnp.float32) - model_image).astype(jnp.bfloat16)
        residual_f = residual.astype(jnp.float32)
        row_level = box_sum(residual_f, RAD, 1)
        level_pad = jnp.pad(row_level, ((RAD, RAD), (0, 0), (0, 0)))
        annulus_total = level_pad[0:height] + level_pad[2 * RAD:2 * RAD + height]
        upright = box_sum(residual_f, RAD - 1, 0)
        side_pad = jnp.pad(upright, ((0, 0), (RAD, RAD), (0, 0)))
        annulus_total = annulus_total + side_pad[:, 0:col_count] + side_pad[:, 2 * RAD:2 * RAD + col_count]
        annulus_fit = annulus_gain[plane_index][None, :, None] * annulus_total / (8.0 * RAD)
        backgrounds.append(annulus_fit.astype(jnp.bfloat16))
        detrended_list.append((residual_f - annulus_fit).astype(jnp.bfloat16))
        frame_step = residual_f[:, :, 1:] - residual_f[:, :, :-1]
        noise_list.append(lax.optimization_barrier(jnp.sum(frame_step * frame_step, axis=2)) / (frame_count - 1))
    traces_out = []
    for plane_index in range(PLANES):
        pooled = 2.0 * noise_list[plane_index]
        if plane_index > 0:
            pooled = pooled + noise_list[plane_index - 1]
        if plane_index + 1 < PLANES:
            pooled = pooled + noise_list[plane_index + 1]
        pooled = pooled / 4.0
        blurred = blur_along(detrended_list[plane_index].astype(jnp.float32), weights, 1)
        smoothed = blur_along(blurred, weights, 0)
        normalized = (smoothed / jnp.sqrt(pooled + noise_eps)[:, :, None]).astype(jnp.bfloat16)

        def project(item_parts):
            tile_values, stripe_value, column_value = item_parts
            start = ((stripe_value * FOOT).astype(jnp.int32), column_value.astype(jnp.int32), jnp.int32(0))
            window = lax.dynamic_slice(normalized, start, (FOOT, FOOT, frame_count))
            return jnp.einsum('yx,yxt->t', tile_values.reshape(FOOT, FOOT).astype(jnp.float32), window.astype(jnp.float32), precision=lax.Precision.HIGHEST)
        gradient = lax.map(project, (footprints[plane_index], stripe[plane_index, :, 0], column[plane_index]))
        foot_f = footprints[plane_index].astype(jnp.float32)
        step_size = 1.0 / (lax.optimization_barrier(jnp.sum(foot_f * foot_f, axis=1)) + norm_eps)
        updated = traces[plane_index].astype(jnp.float32) + step_size[:, None] * gradient
        spikes = deconvolve(updated, decay_slow[plane_index], decay_fast[plane_index])

        def convolve_block(item_parts):
            return reconvolve(item_parts[0], item_parts[1], item_parts[2])
        blocked = lax.map(convolve_block, (spikes.reshape(N_PIX, NEUR_DEV, frame_count), decay_slow[plane_index].reshape(N_PIX, NEUR_DEV), decay_fast[plane_index].reshape(N_PIX, NEUR_DEV)))
        traces_out.append(blocked.reshape(NEUR, frame_count))
    return (jnp.stack(backgrounds), jnp.stack(traces_out))
```

```python
import jax
import jax.numpy as jnp
from jax import lax
from jax.sharding import PartitionSpec as P

FOOT = 32
RAD = 12
GR = 3


lam_floor = 0.1
noise_eps = 1e-05
norm_eps = 1e-05
sigma_twice = 4.5


def with_halo(array, sides, width):
    for axis, dim in sides:
        devices, length = (lax.axis_size(axis), array.shape[dim])
        up = [(i, (i + 1) % devices) for i in range(devices - 1)]
        down = [(j, i) for i, j in up]
        last = lax.slice_in_dim(array, length - width, length, axis=dim)
        initial = lax.slice_in_dim(array, 0, width, axis=dim)
        before = lax.ppermute(last, axis, up)
        after = lax.ppermute(initial, axis, down)
        array = jnp.concatenate([before, array, after], axis=dim)
    return array


def kernel_taps(radius):
    offsets = jnp.arange(-radius, radius + 1).astype(jnp.float32)
    shape_raw = jnp.exp(-offsets * offsets / sigma_twice)
    return (shape_raw / jnp.sum(shape_raw)).astype(jnp.bfloat16)


def deconvolve(updated, decay_slow, decay_fast):
    lag_one = jnp.pad(updated, ((0, 0), (1, 0)))[:, :-1]
    lag_two = jnp.pad(updated, ((0, 0), (2, 0)))[:, :-2]
    driven = (
        updated
        - (decay_slow + decay_fast)[:, None] * lag_one
        + (decay_slow * decay_fast)[:, None] * lag_two
    )
    return jnp.maximum(driven - lam_floor, 0.0)


def reconvolve(spikes, decay_slow, decay_fast):
    frame_count = spikes.shape[1]
    slow_col, fast_col = decay_slow[:, None], decay_fast[:, None]

    def geometric_run(values, ratio):
        total, power, shift = values, ratio, 1
        while shift < frame_count:
            lagged = jnp.pad(total, ((0, 0), (shift, 0)))[:, :-shift]
            total = total + power * lagged
            power = power * power
            shift *= 2
        return total

    slow_run = geometric_run(spikes, slow_col)
    fast_run = geometric_run(spikes, fast_col)
    kernel_scale = (1.0 - decay_slow) * (1.0 - decay_fast) / (decay_slow - decay_fast)
    return kernel_scale[:, None] * (slow_col * slow_run - fast_col * fast_run)


def tap_matrix(out_count, in_count, first_lag, dtype_out):
    gauss_weights = kernel_taps(GR)
    out_index = jnp.arange(out_count)
    in_index = jnp.arange(in_count)
    lag_table = in_index[None, :] - out_index[:, None] - first_lag
    tap_offsets = jnp.arange(2 * GR + 1) - GR
    matches = (lag_table[:, :, None] == tap_offsets[None, None, :]).astype(jnp.bfloat16)
    return jnp.sum(gauss_weights[None, None, :] * matches, axis=2).astype(dtype_out)


def annulus_background(padded_residual, out_count, column_gain):
    col_count = padded_residual.shape[1]
    column_index = jnp.arange(col_count)
    column_band = (jnp.abs(column_index[:, None] - column_index[None, :]) <= RAD).astype(
        jnp.bfloat16
    )
    across = jnp.einsum(
        "rcf,cd->rdf", padded_residual, column_band, preferred_element_type=jnp.float32
    )
    annulus_total = across[0:out_count] + across[2 * RAD : 2 * RAD + out_count]
    out_index = jnp.arange(out_count)
    row_index = jnp.arange(padded_residual.shape[0])
    row_band = (jnp.abs(row_index[None, :] - out_index[:, None] - RAD) <= RAD - 1).astype(
        jnp.bfloat16
    )
    upright = jnp.einsum(
        "or,rcf->ocf", row_band, padded_residual, preferred_element_type=jnp.float32
    )
    side_pad = jnp.pad(upright, ((0, 0), (RAD, RAD), (0, 0)))
    annulus_total = (
        annulus_total + side_pad[:, 0:col_count] + side_pad[:, 2 * RAD : 2 * RAD + col_count]
    )
    return column_gain[None, :, None] * annulus_total / (8.0 * RAD)


def on_device(movie, footprints, traces, stripe, column, annulus_gain, decay_slow, decay_fast):
    pix_count = lax.axis_size("pix")
    row_count = movie.shape[1]
    col_count = movie.shape[2]
    frame_count = movie.shape[3]
    neuron_count = footprints.shape[1]
    capacity = max(2, 2 * neuron_count // pix_count)
    slot_count = pix_count * capacity
    target_stripe = stripe[0, :, 0]
    neuron_index = jnp.arange(neuron_count)
    earlier_same = (target_stripe[:, None] == target_stripe[None, :]) & (
        neuron_index[None, :] < neuron_index[:, None]
    )
    arrival_rank = jnp.sum(earlier_same.astype(jnp.int32), axis=1)
    slot_index = target_stripe * capacity + arrival_rank
    placement = slot_index[:, None] == jnp.arange(slot_count)[None, :]
    placement_b = placement.astype(jnp.bfloat16)
    contract_first = (((0,), (0,)), ((), ()))
    tile_width, trace_width = footprints.shape[2], traces.shape[2]
    column_lanes = jnp.broadcast_to(
        (column[0] + 1).astype(jnp.bfloat16)[:, None], (neuron_count, 128)
    )
    payload = jnp.concatenate([footprints[0], traces[0], column_lanes], axis=1)
    outbox = lax.dot_general(
        placement_b, payload, contract_first, preferred_element_type=jnp.float32
    ).astype(jnp.bfloat16)
    inbox = lax.all_to_all(outbox, "pix", split_axis=0, concat_axis=0, tiled=True)
    tile_inbox = inbox[:, :tile_width]
    trace_inbox = inbox[:, tile_width : tile_width + trace_width]
    column_inbox = inbox[:, tile_width + trace_width].astype(jnp.int32)
    left_edge = column_inbox - 1
    covered = left_edge[:, None] + jnp.arange(FOOT)[None, :]
    column_onehot = (covered[:, :, None] == jnp.arange(col_count)[None, None, :]).astype(
        jnp.bfloat16
    )
    tile_grid = tile_inbox.reshape(slot_count, FOOT, FOOT)
    footprint_rows = (
        jnp.einsum("srj,sjc->src", tile_grid, column_onehot, preferred_element_type=jnp.float32)
        .astype(jnp.bfloat16)
        .reshape(slot_count, FOOT * col_count)
    )
    model_image = lax.dot_general(
        footprint_rows, trace_inbox, contract_first, preferred_element_type=jnp.float32
    )
    residual = (
        movie[0].astype(jnp.float32).reshape(row_count * col_count, frame_count) - model_image
    ).astype(jnp.bfloat16)
    residual = residual.reshape(row_count, col_count, frame_count)
    column_gain = annulus_gain[0]
    padded_residual = with_halo(residual, (("pix", 0),), RAD)
    annulus_fit = annulus_background(padded_residual, row_count, column_gain)
    detrended = (residual.astype(jnp.float32) - annulus_fit).astype(jnp.bfloat16)
    margin_detrended = with_halo(detrended, (("pix", 0),), GR)
    background = annulus_fit.astype(jnp.bfloat16)
    residual_f = residual.astype(jnp.float32)
    frame_step = residual_f[:, :, 1:] - residual_f[:, :, :-1]
    noise_level = jnp.sum(frame_step * frame_step, axis=2) / (frame_count - 1)
    noise_stack = with_halo(noise_level[None], (("plane", 0),), 1)
    pooled = (noise_stack[0] + 2.0 * noise_stack[1] + noise_stack[2]) / 4.0
    column_weights = tap_matrix(col_count, col_count, 0, jnp.bfloat16).T
    blurred = jnp.einsum(
        "rcf,cd->rdf", margin_detrended, column_weights, preferred_element_type=jnp.float32
    )
    row_weights = tap_matrix(row_count, row_count + 2 * GR, GR, jnp.float32)
    smoothed = jnp.einsum("or,rcf->ocf", row_weights, blurred, precision=lax.Precision.HIGHEST)
    normalized = (smoothed / jnp.sqrt(pooled + noise_eps)[:, :, None]).astype(jnp.bfloat16)
    normalized = normalized.reshape(row_count * col_count, frame_count)
    slot_gradient = jnp.dot(footprint_rows, normalized, preferred_element_type=jnp.float32)
    home_gradient = lax.all_to_all(slot_gradient, "pix", split_axis=0, concat_axis=0, tiled=True)
    gradient = lax.dot_general(
        placement.astype(jnp.float32),
        home_gradient,
        (((1,), (0,)), ((), ())),
        precision=lax.Precision.HIGHEST,
    )
    foot_f = footprints[0].astype(jnp.float32)
    step_size = 1.0 / (jnp.sum(foot_f * foot_f, axis=1) + norm_eps)
    updated = traces[0].astype(jnp.float32) + step_size[:, None] * gradient
    spikes = deconvolve(updated, decay_slow[0], decay_fast[0])
    traces_new = reconvolve(spikes, decay_slow[0], decay_fast[0])
    return (background[None], traces_new[None])


def solution(mesh):
    placed = (
        P("plane", "pix", None, None),
        P("plane", "pix", None),
        P("plane", "pix", None),
        P("plane", "pix", None),
        P("plane", "pix"),
        P("plane", None),
        P("plane", "pix"),
        P("plane", "pix"),
    )
    return jax.shard_map(
        on_device,
        mesh=mesh,
        in_specs=placed,
        out_specs=(P("plane", "pix", None, None), P("plane", "pix", None)),
        check_vma=False,
    )
```

```python
import numpy as np
import ml_dtypes
import jax
import jax.numpy as jnp
from jax import lax
from jax.experimental import pallas as pl
from jax.experimental.pallas import tpu as pltpu
from jax.sharding import PartitionSpec as P

FOOT = 32
RAD = 12
GR = 3


lam_floor = 0.1
noise_eps = 1e-05
norm_eps = 1e-05
sigma_twice = 4.5


def with_halo(array, sides, width):
    for axis, dim in sides:
        devices, length = (lax.axis_size(axis), array.shape[dim])
        up = [(i, (i + 1) % devices) for i in range(devices - 1)]
        down = [(j, i) for i, j in up]
        last = lax.slice_in_dim(array, length - width, length, axis=dim)
        initial = lax.slice_in_dim(array, 0, width, axis=dim)
        before = lax.ppermute(last, axis, up)
        after = lax.ppermute(initial, axis, down)
        array = jnp.concatenate([before, array, after], axis=dim)
    return array


def deconvolve(updated, decay_slow, decay_fast):
    lag_one = jnp.pad(updated, ((0, 0), (1, 0)))[:, :-1]
    lag_two = jnp.pad(updated, ((0, 0), (2, 0)))[:, :-2]
    driven = (
        updated
        - (decay_slow + decay_fast)[:, None] * lag_one
        + (decay_slow * decay_fast)[:, None] * lag_two
    )
    return jnp.maximum(driven - lam_floor, 0.0)


def reconvolve(spikes, decay_slow, decay_fast):
    frame_count = spikes.shape[1]
    slow_col, fast_col = decay_slow[:, None], decay_fast[:, None]

    def geometric_run(values, ratio):
        total, power, shift = values, ratio, 1
        while shift < frame_count:
            lagged = jnp.pad(total, ((0, 0), (shift, 0)))[:, :-shift]
            total = total + power * lagged
            power = power * power
            shift *= 2
        return total

    slow_run = geometric_run(spikes, slow_col)
    fast_run = geometric_run(spikes, fast_col)
    kernel_scale = (1.0 - decay_slow) * (1.0 - decay_fast) / (decay_slow - decay_fast)
    return kernel_scale[:, None] * (slow_col * slow_run - fast_col * fast_run)


def tap_values():
    offsets = np.arange(-GR, GR + 1).astype(np.float64)
    raw = np.exp(-offsets * offsets / sigma_twice)
    taps = (raw / raw.sum()).astype(np.float32).astype(ml_dtypes.bfloat16)
    return taps.astype(np.float32)


def band_constants(col_count):
    index = np.arange(col_count)
    gap = index[None, :] - index[:, None]
    box = (np.abs(gap) <= RAD).astype(np.float32)
    side = (np.abs(gap) == RAD).astype(np.float32)
    taps = tap_values()
    blur = np.zeros((col_count, col_count), np.float32)
    for offset in range(-GR, GR + 1):
        blur = blur + np.where(gap == offset, taps[offset + GR], 0.0)
    wcat = np.concatenate([box, side], axis=0).astype(ml_dtypes.bfloat16)
    return wcat, blur.astype(ml_dtypes.bfloat16)


def stencil_kernel(edge_ref, top_ref, own_ref, bot_ref, wcat_ref, blur_ref, gain_ref, denom_ref,
                   back_ref, norm_ref, hsum_ref, ssum_ref, rows_ref):
    halo = top_ref.shape[0]
    own = own_ref.shape[0]
    cols = own_ref.shape[1]
    taps = [float(v) for v in tap_values()]

    def horizontal(e, row):
        prod = jnp.dot(wcat_ref[...], row, preferred_element_type=jnp.float32)
        hsum_ref[e] = prod[:cols]
        ssum_ref[e] = prod[cols:]

    def top_h(r, c):
        horizontal(r, top_ref[r])
        return c

    def own_h(r, c):
        horizontal(halo + r, own_ref[r])
        return c

    def bot_h(r, c):
        horizontal(halo + own + r, bot_ref[r])
        return c

    lax.fori_loop(0, halo, top_h, 0)
    lax.fori_loop(0, own, own_h, 0)
    lax.fori_loop(0, halo, bot_h, 0)

    first = halo - GR
    side = ssum_ref[first - RAD]
    for i in range(1, 2 * RAD - 1):
        side = side + ssum_ref[first - RAD + i]
    gain = gain_ref[...]

    def detrend(k, side, row, keep):
        e = first + k
        side = side + ssum_ref[e + RAD - 1] - ssum_ref[e - RAD]
        total = hsum_ref[e - RAD] + hsum_ref[e + RAD] + side
        fit = gain * total / (8.0 * RAD)
        residual_f = row.astype(jnp.float32)
        det = (residual_f - fit).astype(jnp.bfloat16)
        if keep is not None:
            det = (det.astype(jnp.float32) * keep).astype(jnp.bfloat16)
        rows_ref[k] = jnp.dot(blur_ref[...], det, preferred_element_type=jnp.float32)
        return side, fit

    keep_top = edge_ref[0]
    keep_bot = edge_ref[1]

    def top_d(k, side):
        side, _ = detrend(k, side, top_ref[first + k], keep_top)
        return side

    def own_d(r, side):
        side, fit = detrend(GR + r, side, own_ref[r], None)
        back_ref[r] = fit.astype(back_ref.dtype)
        return side

    def bot_d(r, side):
        side, _ = detrend(GR + own + r, side, bot_ref[r], keep_bot)
        return side

    side = lax.fori_loop(0, GR, top_d, side)
    side = lax.fori_loop(0, own, own_d, side)
    side = lax.fori_loop(0, GR, bot_d, side)

    def smooth(y, c):
        acc = taps[0] * rows_ref[y]
        for o in range(1, 2 * GR + 1):
            acc = acc + taps[o] * rows_ref[y + o]
        norm_ref[y] = (acc / denom_ref[y]).astype(norm_ref.dtype)
        return c

    lax.fori_loop(0, own, smooth, 0)


def stencil(edge, top, own, bot, gain_col, denom, frame_block=128):
    halo, own_rows, cols, frames = top.shape[0], own.shape[0], own.shape[1], own.shape[2]
    ext = 2 * halo + own_rows
    wcat, blur = band_constants(cols)
    grid = (frames // frame_block,)
    row_block = lambda n: pl.BlockSpec((n, cols, frame_block), lambda j: (0, 0, j))
    fixed = lambda shape: pl.BlockSpec(shape, lambda j: (0,) * len(shape))
    return pl.pallas_call(
        stencil_kernel,
        grid=grid,
        in_specs=[
            pl.BlockSpec(memory_space=pltpu.SMEM),
            row_block(halo), row_block(own_rows), row_block(halo),
            fixed((2 * cols, cols)), fixed((cols, cols)), fixed((cols, 1)), fixed((own_rows, cols, 1)),
        ],
        out_specs=[row_block(own_rows), row_block(own_rows)],
        out_shape=[jax.ShapeDtypeStruct(own.shape, jnp.bfloat16), jax.ShapeDtypeStruct(own.shape, jnp.bfloat16)],
        scratch_shapes=[
            pltpu.VMEM((ext, cols, frame_block), jnp.float32),
            pltpu.VMEM((ext, cols, frame_block), jnp.float32),
            pltpu.VMEM((own_rows + 2 * GR, cols, frame_block), jnp.float32),
        ],
        compiler_params=pltpu.CompilerParams(vmem_limit_bytes=60 * 1024 * 1024),
    )(edge, top, own, bot, jnp.asarray(wcat), jnp.asarray(blur), gain_col, denom)


def on_device(movie, footprints, traces, stripe, column, annulus_gain, decay_slow, decay_fast):
    pix_count = lax.axis_size("pix")
    row_count = movie.shape[1]
    col_count = movie.shape[2]
    frame_count = movie.shape[3]
    neuron_count = footprints.shape[1]
    capacity = max(2, 2 * neuron_count // pix_count)
    slot_count = pix_count * capacity
    target_stripe = stripe[0, :, 0]
    neuron_index = jnp.arange(neuron_count)
    earlier_same = (target_stripe[:, None] == target_stripe[None, :]) & (
        neuron_index[None, :] < neuron_index[:, None]
    )
    arrival_rank = jnp.sum(earlier_same.astype(jnp.int32), axis=1)
    slot_index = target_stripe * capacity + arrival_rank
    placement = slot_index[:, None] == jnp.arange(slot_count)[None, :]
    placement_b = placement.astype(jnp.bfloat16)
    contract_first = (((0,), (0,)), ((), ()))
    tile_width, trace_width = footprints.shape[2], traces.shape[2]
    column_lanes = jnp.broadcast_to(
        (column[0] + 1).astype(jnp.bfloat16)[:, None], (neuron_count, 128)
    )
    payload = jnp.concatenate([footprints[0], traces[0], column_lanes], axis=1)
    outbox = lax.dot_general(
        placement_b, payload, contract_first, preferred_element_type=jnp.float32
    ).astype(jnp.bfloat16)
    inbox = lax.all_to_all(outbox, "pix", split_axis=0, concat_axis=0, tiled=True)
    tile_inbox = inbox[:, :tile_width]
    trace_inbox = inbox[:, tile_width : tile_width + trace_width]
    column_inbox = inbox[:, tile_width + trace_width].astype(jnp.int32)
    left_edge = column_inbox - 1
    covered = left_edge[:, None] + jnp.arange(FOOT)[None, :]
    column_onehot = (covered[:, :, None] == jnp.arange(col_count)[None, None, :]).astype(
        jnp.bfloat16
    )
    tile_grid = tile_inbox.reshape(slot_count, FOOT, FOOT)
    footprint_rows = (
        jnp.einsum("srj,sjc->src", tile_grid, column_onehot, preferred_element_type=jnp.float32)
        .astype(jnp.bfloat16)
        .reshape(slot_count, FOOT * col_count)
    )
    model_image = lax.dot_general(
        footprint_rows, trace_inbox, contract_first, preferred_element_type=jnp.float32
    )
    residual = (
        movie[0].astype(jnp.float32).reshape(row_count * col_count, frame_count) - model_image
    ).astype(jnp.bfloat16)
    residual = residual.reshape(row_count, col_count, frame_count)
    halo = RAD + GR
    pix_index = lax.axis_index("pix")
    up = [(i, i + 1) for i in range(pix_count - 1)]
    down = [(j, i) for i, j in up]
    top_halo = lax.ppermute(residual[row_count - halo :], "pix", up)
    bottom_halo = lax.ppermute(residual[:halo], "pix", down)
    residual_f = residual.astype(jnp.float32)
    frame_step = residual_f[:, :, 1:] - residual_f[:, :, :-1]
    noise_level = jnp.sum(frame_step * frame_step, axis=2) / (frame_count - 1)
    noise_stack = with_halo(noise_level[None], (("plane", 0),), 1)
    pooled = (noise_stack[0] + 2.0 * noise_stack[1] + noise_stack[2]) / 4.0
    denom = jnp.sqrt(pooled + noise_eps)[:, :, None]
    edge = jnp.stack([pix_index > 0, pix_index < pix_count - 1]).astype(jnp.float32)
    background, normalized = stencil(
        edge, top_halo, residual, bottom_halo, annulus_gain[0][:, None], denom
    )
    normalized = normalized.reshape(row_count * col_count, frame_count)
    slot_gradient = jnp.dot(footprint_rows, normalized, preferred_element_type=jnp.float32)
    home_gradient = lax.all_to_all(slot_gradient, "pix", split_axis=0, concat_axis=0, tiled=True)
    gradient = lax.dot_general(
        placement.astype(jnp.float32),
        home_gradient,
        (((1,), (0,)), ((), ())),
        precision=lax.Precision.HIGHEST,
    )
    foot_f = footprints[0].astype(jnp.float32)
    step_size = 1.0 / (jnp.sum(foot_f * foot_f, axis=1) + norm_eps)
    updated = traces[0].astype(jnp.float32) + step_size[:, None] * gradient
    spikes = deconvolve(updated, decay_slow[0], decay_fast[0])
    traces_new = reconvolve(spikes, decay_slow[0], decay_fast[0])
    return (background[None], traces_new[None])


def solution(mesh):
    placed = (
        P("plane", "pix", None, None),
        P("plane", "pix", None),
        P("plane", "pix", None),
        P("plane", "pix", None),
        P("plane", "pix"),
        P("plane", None),
        P("plane", "pix"),
        P("plane", "pix"),
    )
    return jax.shard_map(
        on_device,
        mesh=mesh,
        in_specs=placed,
        out_specs=(P("plane", "pix", None, None), P("plane", "pix", None)),
        check_vma=False,
    )
```

```python
import numpy as np
import ml_dtypes
import jax
import jax.numpy as jnp
from jax import lax
from jax.experimental import pallas as pl
from jax.experimental.pallas import tpu as pltpu
from jax.sharding import PartitionSpec as P

FOOT = 32
RAD = 12
GR = 3


lam_floor = 0.1
noise_eps = 1e-05
norm_eps = 1e-05
sigma_twice = 4.5


def with_halo(array, sides, width):
    for axis, dim in sides:
        devices, length = (lax.axis_size(axis), array.shape[dim])
        up = [(i, (i + 1) % devices) for i in range(devices - 1)]
        down = [(j, i) for i, j in up]
        last = lax.slice_in_dim(array, length - width, length, axis=dim)
        initial = lax.slice_in_dim(array, 0, width, axis=dim)
        before = lax.ppermute(last, axis, up)
        after = lax.ppermute(initial, axis, down)
        array = jnp.concatenate([before, array, after], axis=dim)
    return array


def deconvolve(updated, decay_slow, decay_fast):
    lag_one = jnp.pad(updated, ((0, 0), (1, 0)))[:, :-1]
    lag_two = jnp.pad(updated, ((0, 0), (2, 0)))[:, :-2]
    driven = (
        updated
        - (decay_slow + decay_fast)[:, None] * lag_one
        + (decay_slow * decay_fast)[:, None] * lag_two
    )
    return jnp.maximum(driven - lam_floor, 0.0)


def reconvolve(spikes, decay_slow, decay_fast):
    frame_count = spikes.shape[1]
    slow_col, fast_col = decay_slow[:, None], decay_fast[:, None]

    def geometric_run(values, ratio):
        total, power, shift = values, ratio, 1
        while shift < frame_count:
            lagged = jnp.pad(total, ((0, 0), (shift, 0)))[:, :-shift]
            total = total + power * lagged
            power = power * power
            shift *= 2
        return total

    slow_run = geometric_run(spikes, slow_col)
    fast_run = geometric_run(spikes, fast_col)
    kernel_scale = (1.0 - decay_slow) * (1.0 - decay_fast) / (decay_slow - decay_fast)
    return kernel_scale[:, None] * (slow_col * slow_run - fast_col * fast_run)


def tap_values():
    offsets = np.arange(-GR, GR + 1).astype(np.float64)
    raw = np.exp(-offsets * offsets / sigma_twice)
    taps = (raw / raw.sum()).astype(np.float32).astype(ml_dtypes.bfloat16)
    return taps.astype(np.float32)


def band_constants(col_count):
    index = np.arange(col_count)
    gap = index[None, :] - index[:, None]
    box = (np.abs(gap) <= RAD).astype(np.float32)
    side = (np.abs(gap) == RAD).astype(np.float32)
    taps = tap_values()
    blur = np.zeros((col_count, col_count), np.float32)
    for offset in range(-GR, GR + 1):
        blur = blur + np.where(gap == offset, taps[offset + GR], 0.0)
    wcat = np.concatenate([box, side], axis=0).astype(ml_dtypes.bfloat16)
    return wcat, blur.astype(ml_dtypes.bfloat16)


def stencil_kernel(edge_ref, top_ref, own_ref, bot_ref, wcat_ref, blur_ref, scale_ref, recip_ref,
                   frows_ref, back_ref, grad_ref, hsum_ref, ssum_ref, rows_ref):
    halo = top_ref.shape[0]
    own = own_ref.shape[0]
    cols = own_ref.shape[1]
    taps = [float(v) for v in tap_values()]

    def horizontal(e, row):
        prod = jnp.dot(wcat_ref[...], row, preferred_element_type=jnp.float32)
        hsum_ref[e] = prod[:cols]
        ssum_ref[e] = prod[cols:]

    def top_h(r, c):
        horizontal(r, top_ref[r])
        return c

    def own_h(r, c):
        horizontal(halo + r, own_ref[r])
        return c

    def bot_h(r, c):
        horizontal(halo + own + r, bot_ref[r])
        return c

    lax.fori_loop(0, halo, top_h, 0)
    lax.fori_loop(0, own, own_h, 0)
    lax.fori_loop(0, halo, bot_h, 0)

    first = halo - GR
    side = ssum_ref[first - RAD]
    for i in range(1, 2 * RAD - 1):
        side = side + ssum_ref[first - RAD + i]

    def detrend(k, side, row, keep):
        e = first + k
        side = side + ssum_ref[e + RAD - 1] - ssum_ref[e - RAD]
        total = hsum_ref[e - RAD] + hsum_ref[e + RAD] + side
        fit = scale_ref[...] * total
        residual_f = row.astype(jnp.float32)
        det = (residual_f - fit).astype(jnp.bfloat16)
        if keep is not None:
            det = (det.astype(jnp.float32) * keep).astype(jnp.bfloat16)
        rows_ref[k] = jnp.dot(blur_ref[...], det, preferred_element_type=jnp.float32)
        return side, fit

    keep_top = edge_ref[0]
    keep_bot = edge_ref[1]

    def top_d(k, side):
        side, _ = detrend(k, side, top_ref[first + k], keep_top)
        return side

    def own_d(r, side):
        side, fit = detrend(GR + r, side, own_ref[r], None)
        back_ref[r] = fit.astype(back_ref.dtype)
        return side

    def bot_d(r, side):
        side, _ = detrend(GR + own + r, side, bot_ref[r], keep_bot)
        return side

    side = lax.fori_loop(0, GR, top_d, side)
    side = lax.fori_loop(0, own, own_d, side)
    side = lax.fori_loop(0, GR, bot_d, side)

    grad_ref[...] = jnp.zeros_like(grad_ref)

    def smooth(y, c):
        acc = taps[GR] * rows_ref[y + GR]
        for o in range(GR):
            acc = acc + taps[o] * (rows_ref[y + o] + rows_ref[y + 2 * GR - o])
        normalized = (acc * recip_ref[y]).astype(jnp.bfloat16)
        grad_ref[...] += jnp.dot(frows_ref[y], normalized, preferred_element_type=jnp.float32)
        return c

    lax.fori_loop(0, own, smooth, 0)


def stencil(edge, top, own, bot, scale, recip, frows, frame_block=128):
    halo, own_rows, cols, frames = top.shape[0], own.shape[0], own.shape[1], own.shape[2]
    slots = frows.shape[1]
    ext = 2 * halo + own_rows
    wcat, blur = band_constants(cols)
    grid = (frames // frame_block,)
    row_block = lambda n: pl.BlockSpec((n, cols, frame_block), lambda j: (0, 0, j))
    fixed = lambda shape: pl.BlockSpec(shape, lambda j: (0,) * len(shape))
    return pl.pallas_call(
        stencil_kernel,
        grid=grid,
        in_specs=[
            pl.BlockSpec(memory_space=pltpu.SMEM),
            row_block(halo), row_block(own_rows), row_block(halo),
            fixed((2 * cols, cols)), fixed((cols, cols)), fixed((cols, frame_block)),
            fixed((own_rows, cols, frame_block)), fixed((own_rows, slots, cols)),
        ],
        out_specs=[row_block(own_rows), pl.BlockSpec((slots, frame_block), lambda j: (0, j))],
        out_shape=[jax.ShapeDtypeStruct(own.shape, jnp.bfloat16),
                   jax.ShapeDtypeStruct((slots, frames), jnp.float32)],
        scratch_shapes=[
            pltpu.VMEM((ext, cols, frame_block), jnp.float32),
            pltpu.VMEM((ext, cols, frame_block), jnp.float32),
            pltpu.VMEM((own_rows + 2 * GR, cols, frame_block), jnp.float32),
        ],
        compiler_params=pltpu.CompilerParams(vmem_limit_bytes=60 * 1024 * 1024),
    )(edge, top, own, bot, jnp.asarray(wcat), jnp.asarray(blur), scale, recip, frows)


def on_device(movie, footprints, traces, stripe, column, annulus_gain, decay_slow, decay_fast):
    pix_count = lax.axis_size("pix")
    row_count = movie.shape[1]
    col_count = movie.shape[2]
    frame_count = movie.shape[3]
    neuron_count = footprints.shape[1]
    capacity = max(2, 2 * neuron_count // pix_count)
    slot_count = pix_count * capacity
    target_stripe = stripe[0, :, 0]
    neuron_index = jnp.arange(neuron_count)
    earlier_same = (target_stripe[:, None] == target_stripe[None, :]) & (
        neuron_index[None, :] < neuron_index[:, None]
    )
    arrival_rank = jnp.sum(earlier_same.astype(jnp.int32), axis=1)
    slot_index = target_stripe * capacity + arrival_rank
    placement = slot_index[:, None] == jnp.arange(slot_count)[None, :]
    placement_b = placement.astype(jnp.bfloat16)
    contract_first = (((0,), (0,)), ((), ()))
    tile_width, trace_width = footprints.shape[2], traces.shape[2]
    column_lanes = jnp.broadcast_to(
        (column[0] + 1).astype(jnp.bfloat16)[:, None], (neuron_count, 128)
    )
    payload = jnp.concatenate([footprints[0], traces[0], column_lanes], axis=1)
    outbox = lax.dot_general(
        placement_b, payload, contract_first, preferred_element_type=jnp.float32
    ).astype(jnp.bfloat16)
    inbox = lax.all_to_all(outbox, "pix", split_axis=0, concat_axis=0, tiled=True)
    tile_inbox = inbox[:, :tile_width]
    trace_inbox = inbox[:, tile_width : tile_width + trace_width]
    column_inbox = inbox[:, tile_width + trace_width].astype(jnp.int32)
    left_edge = column_inbox - 1
    covered = left_edge[:, None] + jnp.arange(FOOT)[None, :]
    column_onehot = (covered[:, :, None] == jnp.arange(col_count)[None, None, :]).astype(
        jnp.bfloat16
    )
    tile_grid = tile_inbox.reshape(slot_count, FOOT, FOOT)
    frows = jnp.einsum(
        "srj,sjc->rsc", tile_grid, column_onehot, preferred_element_type=jnp.float32
    ).astype(jnp.bfloat16)
    model_image = jnp.einsum(
        "rsc,st->rct", frows, trace_inbox, preferred_element_type=jnp.float32
    )
    residual = (movie[0].astype(jnp.float32) - model_image).astype(jnp.bfloat16)
    halo = RAD + GR
    pix_index = lax.axis_index("pix")
    up = [(i, i + 1) for i in range(pix_count - 1)]
    down = [(j, i) for i, j in up]
    top_halo = lax.ppermute(residual[row_count - halo :], "pix", up)
    bottom_halo = lax.ppermute(residual[:halo], "pix", down)
    frame_index = np.arange(frame_count)
    step_matrix = (
        (frame_index[:, None] == frame_index[None, :] + 1).astype(np.float32)
        - (frame_index[:, None] == frame_index[None, :]).astype(np.float32)
    ) * (frame_index[None, :] < frame_count - 1)
    frame_step = jnp.dot(
        residual.reshape(row_count * col_count, frame_count),
        jnp.asarray(step_matrix, jnp.bfloat16),
        preferred_element_type=jnp.float32,
    )
    noise_level = (jnp.sum(frame_step * frame_step, axis=1) / (frame_count - 1)).reshape(
        row_count, col_count
    )
    noise_stack = with_halo(noise_level[None], (("plane", 0),), 1)
    pooled = (noise_stack[0] + 2.0 * noise_stack[1] + noise_stack[2]) / 4.0
    frame_block = 128
    recip = jnp.broadcast_to(
        (1.0 / jnp.sqrt(pooled + noise_eps))[:, :, None], (row_count, col_count, frame_block)
    )
    scale = jnp.broadcast_to((annulus_gain[0] / (8.0 * RAD))[:, None], (col_count, frame_block))
    edge = jnp.stack([pix_index > 0, pix_index < pix_count - 1]).astype(jnp.float32)
    background, slot_gradient = stencil(
        edge, top_halo, residual, bottom_halo, scale, recip, frows, frame_block
    )
    home_gradient = lax.all_to_all(slot_gradient, "pix", split_axis=0, concat_axis=0, tiled=True)
    gradient = lax.dot_general(
        placement.astype(jnp.float32),
        home_gradient,
        (((1,), (0,)), ((), ())),
        precision=lax.Precision.HIGHEST,
    )
    foot_f = footprints[0].astype(jnp.float32)
    step_size = 1.0 / (jnp.sum(foot_f * foot_f, axis=1) + norm_eps)
    updated = traces[0].astype(jnp.float32) + step_size[:, None] * gradient
    spikes = deconvolve(updated, decay_slow[0], decay_fast[0])
    traces_new = reconvolve(spikes, decay_slow[0], decay_fast[0])
    return (background[None], traces_new[None])


def solution(mesh):
    placed = (
        P("plane", "pix", None, None),
        P("plane", "pix", None),
        P("plane", "pix", None),
        P("plane", "pix", None),
        P("plane", "pix"),
        P("plane", None),
        P("plane", "pix"),
        P("plane", "pix"),
    )
    return jax.shard_map(
        on_device,
        mesh=mesh,
        in_specs=placed,
        out_specs=(P("plane", "pix", None, None), P("plane", "pix", None)),
        check_vma=False,
    )
```

```python
import functools
import numpy as np
import ml_dtypes
import jax
import jax.numpy as jnp
from jax import lax
from jax.experimental import pallas as pl
from jax.experimental.pallas import tpu as pltpu
from jax.sharding import PartitionSpec as P

FOOT = 32
RAD = 12
GR = 3


lam_floor = 0.1
noise_eps = 1e-05
norm_eps = 1e-05
sigma_twice = 4.5


def with_halo(array, sides, width):
    for axis, dim in sides:
        devices, length = (lax.axis_size(axis), array.shape[dim])
        up = [(i, (i + 1) % devices) for i in range(devices - 1)]
        down = [(j, i) for i, j in up]
        last = lax.slice_in_dim(array, length - width, length, axis=dim)
        initial = lax.slice_in_dim(array, 0, width, axis=dim)
        before = lax.ppermute(last, axis, up)
        after = lax.ppermute(initial, axis, down)
        array = jnp.concatenate([before, array, after], axis=dim)
    return array


def deconvolve(updated, decay_slow, decay_fast):
    lag_one = jnp.pad(updated, ((0, 0), (1, 0)))[:, :-1]
    lag_two = jnp.pad(updated, ((0, 0), (2, 0)))[:, :-2]
    driven = (
        updated
        - (decay_slow + decay_fast)[:, None] * lag_one
        + (decay_slow * decay_fast)[:, None] * lag_two
    )
    return jnp.maximum(driven - lam_floor, 0.0)


def reconvolve(spikes, decay_slow, decay_fast):
    frame_count = spikes.shape[1]
    slow_col, fast_col = decay_slow[:, None], decay_fast[:, None]

    def geometric_run(values, ratio):
        total, power, shift = values, ratio, 1
        while shift < frame_count:
            lagged = jnp.pad(total, ((0, 0), (shift, 0)))[:, :-shift]
            total = total + power * lagged
            power = power * power
            shift *= 2
        return total

    slow_run = geometric_run(spikes, slow_col)
    fast_run = geometric_run(spikes, fast_col)
    kernel_scale = (1.0 - decay_slow) * (1.0 - decay_fast) / (decay_slow - decay_fast)
    return kernel_scale[:, None] * (slow_col * slow_run - fast_col * fast_run)


def tap_values():
    offsets = np.arange(-GR, GR + 1).astype(np.float64)
    raw = np.exp(-offsets * offsets / sigma_twice)
    taps = (raw / raw.sum()).astype(np.float32).astype(ml_dtypes.bfloat16)
    return taps.astype(np.float32)


def band_constants(col_count):
    index = np.arange(col_count)
    gap = index[None, :] - index[:, None]
    box = (np.abs(gap) <= RAD).astype(np.float32)
    side = (np.abs(gap) == RAD).astype(np.float32)
    taps = tap_values()
    blur = np.zeros((col_count, col_count), np.float32)
    for offset in range(-GR, GR + 1):
        blur = blur + np.where(gap == offset, taps[offset + GR], 0.0)
    wcat = np.concatenate([box, side], axis=0).astype(ml_dtypes.bfloat16)
    return wcat, blur.astype(ml_dtypes.bfloat16)


def stencil_kernel(edge_ref, top_ref, own_ref, bot_ref, wcat_ref, blur_ref, scale_ref, recip_ref,
                   frows_ref, back_ref, grad_ref, hsum_ref, ssum_ref, rows_ref):
    halo = top_ref.shape[0]
    own = own_ref.shape[0]
    cols = own_ref.shape[1]
    taps = [float(v) for v in tap_values()]

    def horizontal(e, row):
        prod = jnp.dot(wcat_ref[...], row, preferred_element_type=jnp.float32)
        hsum_ref[e] = prod[:cols]
        ssum_ref[e] = prod[cols:]

    def top_h(r, c):
        horizontal(r, top_ref[r])
        return c

    def own_h(r, c):
        horizontal(halo + r, own_ref[r])
        return c

    def bot_h(r, c):
        horizontal(halo + own + r, bot_ref[r])
        return c

    lax.fori_loop(0, halo, top_h, 0)
    lax.fori_loop(0, own, own_h, 0)
    lax.fori_loop(0, halo, bot_h, 0)

    first = halo - GR
    side = ssum_ref[first - RAD]
    for i in range(1, 2 * RAD - 1):
        side = side + ssum_ref[first - RAD + i]

    def detrend(k, side, row, keep):
        e = first + k
        side = side + ssum_ref[e + RAD - 1] - ssum_ref[e - RAD]
        total = hsum_ref[e - RAD] + hsum_ref[e + RAD] + side
        fit = scale_ref[...] * total
        residual_f = row.astype(jnp.float32)
        det = (residual_f - fit).astype(jnp.bfloat16)
        if keep is not None:
            det = (det.astype(jnp.float32) * keep).astype(jnp.bfloat16)
        rows_ref[k] = jnp.dot(blur_ref[...], det, preferred_element_type=jnp.float32)
        return side, fit

    keep_top = edge_ref[0]
    keep_bot = edge_ref[1]

    def top_d(k, side):
        side, _ = detrend(k, side, top_ref[first + k], keep_top)
        return side

    def own_d(r, side):
        side, fit = detrend(GR + r, side, own_ref[r], None)
        back_ref[r] = fit.astype(back_ref.dtype)
        return side

    def bot_d(r, side):
        side, _ = detrend(GR + own + r, side, bot_ref[r], keep_bot)
        return side

    side = lax.fori_loop(0, GR, top_d, side)
    side = lax.fori_loop(0, own, own_d, side)
    side = lax.fori_loop(0, GR, bot_d, side)

    grad_ref[...] = jnp.zeros_like(grad_ref)

    def smooth(y, c):
        acc = taps[GR] * rows_ref[y + GR]
        for o in range(GR):
            acc = acc + taps[o] * (rows_ref[y + o] + rows_ref[y + 2 * GR - o])
        normalized = (acc * recip_ref[y]).astype(jnp.bfloat16)
        grad_ref[...] += jnp.dot(frows_ref[y], normalized, preferred_element_type=jnp.float32)
        return c

    lax.fori_loop(0, own, smooth, 0)


def stencil(edge, top, own, bot, scale, recip, frows, frame_block=128):
    halo, own_rows, cols, frames = top.shape[0], own.shape[0], own.shape[1], own.shape[2]
    slots = frows.shape[1]
    ext = 2 * halo + own_rows
    wcat, blur = band_constants(cols)
    grid = (frames // frame_block,)
    row_block = lambda n: pl.BlockSpec((n, cols, frame_block), lambda j: (0, 0, j))
    fixed = lambda shape: pl.BlockSpec(shape, lambda j: (0,) * len(shape))
    return pl.pallas_call(
        stencil_kernel,
        grid=grid,
        in_specs=[
            pl.BlockSpec(memory_space=pltpu.SMEM),
            row_block(halo), row_block(own_rows), row_block(halo),
            fixed((2 * cols, cols)), fixed((cols, cols)), fixed((cols, frame_block)),
            fixed((own_rows, cols, frame_block)), fixed((own_rows, slots, cols)),
        ],
        out_specs=[row_block(own_rows), pl.BlockSpec((slots, frame_block), lambda j: (0, j))],
        out_shape=[jax.ShapeDtypeStruct(own.shape, jnp.bfloat16),
                   jax.ShapeDtypeStruct((slots, frames), jnp.float32)],
        scratch_shapes=[
            pltpu.VMEM((ext, cols, frame_block), jnp.float32),
            pltpu.VMEM((ext, cols, frame_block), jnp.float32),
            pltpu.VMEM((own_rows + 2 * GR, cols, frame_block), jnp.float32),
        ],
        compiler_params=pltpu.CompilerParams(vmem_limit_bytes=60 * 1024 * 1024),
    )(edge, top, own, bot, jnp.asarray(wcat), jnp.asarray(blur), scale, recip, frows)


MESH = pl.DeviceIdType.MESH


def exchange_kernel(out_ref, in_ref, send_sem, recv_sem, local_sem):
    count = out_ref.shape[0]
    me = lax.axis_index("pix")
    barrier = pltpu.get_barrier_semaphore()

    def peer_at(k):
        return lax.rem(me + k, count)

    def source_at(k):
        return lax.rem(me + count - k, count)

    def remote(target, block):
        return pltpu.make_async_remote_copy(
            src_ref=out_ref.at[target],
            dst_ref=in_ref.at[block],
            send_sem=send_sem.at[target],
            recv_sem=recv_sem.at[block],
            device_id={"pix": target},
            device_id_type=MESH,
        )

    def greet(k, c):
        pl.semaphore_signal(barrier, inc=1, device_id={"pix": peer_at(k)}, device_id_type=MESH)
        return c

    lax.fori_loop(1, count, greet, 0)
    pl.semaphore_wait(barrier, count - 1)

    def launch(k, c):
        remote(peer_at(k), me).start()
        return c

    lax.fori_loop(1, count, launch, 0)
    local = pltpu.make_async_copy(out_ref.at[me], in_ref.at[me], local_sem)
    local.start()
    local.wait()

    def finish(k, c):
        remote(peer_at(k), me).wait_send()
        remote(source_at(k), source_at(k)).wait_recv()
        return c

    lax.fori_loop(1, count, finish, 0)


def exchange(outbox, collective):
    count = outbox.shape[0]
    return pl.pallas_call(
        exchange_kernel,
        out_shape=jax.ShapeDtypeStruct(outbox.shape, outbox.dtype),
        in_specs=[pl.BlockSpec(memory_space=pl.ANY)],
        out_specs=pl.BlockSpec(memory_space=pl.ANY),
        scratch_shapes=[
            pltpu.SemaphoreType.DMA((count,)),
            pltpu.SemaphoreType.DMA((count,)),
            pltpu.SemaphoreType.DMA,
        ],
        compiler_params=pltpu.CompilerParams(collective_id=collective, has_side_effects=True),
    )(outbox)


def on_device(movie, footprints, traces, stripe, column, annulus_gain, decay_slow, decay_fast):
    pix_count = lax.axis_size("pix")
    row_count = movie.shape[1]
    col_count = movie.shape[2]
    frame_count = movie.shape[3]
    neuron_count = footprints.shape[1]
    capacity = max(2, 2 * neuron_count // pix_count)
    slot_count = pix_count * capacity
    target_stripe = stripe[0, :, 0]
    neuron_index = jnp.arange(neuron_count)
    earlier_same = (target_stripe[:, None] == target_stripe[None, :]) & (
        neuron_index[None, :] < neuron_index[:, None]
    )
    arrival_rank = jnp.sum(earlier_same.astype(jnp.int32), axis=1)
    slot_index = target_stripe * capacity + arrival_rank
    placement = slot_index[:, None] == jnp.arange(slot_count)[None, :]
    placement_b = placement.astype(jnp.bfloat16)
    contract_first = (((0,), (0,)), ((), ()))
    tile_width, trace_width = footprints.shape[2], traces.shape[2]
    column_lanes = jnp.broadcast_to(
        (column[0] + 1).astype(jnp.bfloat16)[:, None], (neuron_count, 128)
    )
    payload = jnp.concatenate([footprints[0], traces[0], column_lanes], axis=1)
    outbox = lax.dot_general(
        placement_b, payload, contract_first, preferred_element_type=jnp.float32
    ).astype(jnp.bfloat16)
    inbox = exchange(outbox.reshape(pix_count, capacity, -1), 0).reshape(slot_count, -1)
    tile_inbox = inbox[:, :tile_width]
    trace_inbox = inbox[:, tile_width : tile_width + trace_width]
    column_inbox = inbox[:, tile_width + trace_width].astype(jnp.int32)
    left_edge = column_inbox - 1
    covered = left_edge[:, None] + jnp.arange(FOOT)[None, :]
    column_onehot = (covered[:, :, None] == jnp.arange(col_count)[None, None, :]).astype(
        jnp.bfloat16
    )
    tile_grid = tile_inbox.reshape(slot_count, FOOT, FOOT)
    frows = jnp.einsum(
        "srj,sjc->rsc", tile_grid, column_onehot, preferred_element_type=jnp.float32
    ).astype(jnp.bfloat16)
    model_image = jnp.einsum(
        "rsc,st->rct", frows, trace_inbox, preferred_element_type=jnp.float32
    )
    residual = (movie[0].astype(jnp.float32) - model_image).astype(jnp.bfloat16)
    halo = RAD + GR
    pix_index = lax.axis_index("pix")
    up = [(i, i + 1) for i in range(pix_count - 1)]
    down = [(j, i) for i, j in up]
    top_halo = lax.ppermute(residual[row_count - halo :], "pix", up)
    bottom_halo = lax.ppermute(residual[:halo], "pix", down)
    frame_index = np.arange(frame_count)
    step_matrix = (
        (frame_index[:, None] == frame_index[None, :] + 1).astype(np.float32)
        - (frame_index[:, None] == frame_index[None, :]).astype(np.float32)
    ) * (frame_index[None, :] < frame_count - 1)
    frame_step = jnp.dot(
        residual.reshape(row_count * col_count, frame_count),
        jnp.asarray(step_matrix, jnp.bfloat16),
        preferred_element_type=jnp.float32,
    )
    noise_level = (jnp.sum(frame_step * frame_step, axis=1) / (frame_count - 1)).reshape(
        row_count, col_count
    )
    noise_stack = with_halo(noise_level[None], (("plane", 0),), 1)
    pooled = (noise_stack[0] + 2.0 * noise_stack[1] + noise_stack[2]) / 4.0
    frame_block = 128
    recip = jnp.broadcast_to(
        (1.0 / jnp.sqrt(pooled + noise_eps))[:, :, None], (row_count, col_count, frame_block)
    )
    scale = jnp.broadcast_to((annulus_gain[0] / (8.0 * RAD))[:, None], (col_count, frame_block))
    edge = jnp.stack([pix_index > 0, pix_index < pix_count - 1]).astype(jnp.float32)
    background, slot_gradient = stencil(
        edge, top_halo, residual, bottom_halo, scale, recip, frows, frame_block
    )
    home_gradient = exchange(slot_gradient.reshape(pix_count, capacity, -1), 1).reshape(
        slot_count, -1
    )
    gradient = lax.dot_general(
        placement.astype(jnp.float32),
        home_gradient,
        (((1,), (0,)), ((), ())),
        precision=lax.Precision.HIGHEST,
    )
    foot_f = footprints[0].astype(jnp.float32)
    step_size = 1.0 / (jnp.sum(foot_f * foot_f, axis=1) + norm_eps)
    updated = traces[0].astype(jnp.float32) + step_size[:, None] * gradient
    spikes = deconvolve(updated, decay_slow[0], decay_fast[0])
    traces_new = reconvolve(spikes, decay_slow[0], decay_fast[0])
    return (background[None], traces_new[None])


def solution(mesh):
    placed = (
        P("plane", "pix", None, None),
        P("plane", "pix", None),
        P("plane", "pix", None),
        P("plane", "pix", None),
        P("plane", "pix"),
        P("plane", None),
        P("plane", "pix"),
        P("plane", "pix"),
    )
    return jax.shard_map(
        on_device,
        mesh=mesh,
        in_specs=placed,
        out_specs=(P("plane", "pix", None, None), P("plane", "pix", None)),
        check_vma=False,
    )
```

```python
import functools
import numpy as np
import ml_dtypes
import jax
import jax.numpy as jnp
from jax import lax
from jax.experimental import pallas as pl
from jax.experimental.pallas import tpu as pltpu
from jax.sharding import PartitionSpec as P

FOOT = 32
RAD = 12
GR = 3


lam_floor = 0.1
noise_eps = 1e-05
norm_eps = 1e-05
sigma_twice = 4.5


def with_halo(array, sides, width):
    for axis, dim in sides:
        devices, length = (lax.axis_size(axis), array.shape[dim])
        up = [(i, (i + 1) % devices) for i in range(devices - 1)]
        down = [(j, i) for i, j in up]
        last = lax.slice_in_dim(array, length - width, length, axis=dim)
        initial = lax.slice_in_dim(array, 0, width, axis=dim)
        before = lax.ppermute(last, axis, up)
        after = lax.ppermute(initial, axis, down)
        array = jnp.concatenate([before, array, after], axis=dim)
    return array


def deconvolve(updated, decay_slow, decay_fast):
    lag_one = jnp.pad(updated, ((0, 0), (1, 0)))[:, :-1]
    lag_two = jnp.pad(updated, ((0, 0), (2, 0)))[:, :-2]
    driven = (
        updated
        - (decay_slow + decay_fast)[:, None] * lag_one
        + (decay_slow * decay_fast)[:, None] * lag_two
    )
    return jnp.maximum(driven - lam_floor, 0.0)


def reconvolve(spikes, decay_slow, decay_fast):
    frame_count = spikes.shape[1]
    slow_col, fast_col = decay_slow[:, None], decay_fast[:, None]

    def geometric_run(values, ratio):
        total, power, shift = values, ratio, 1
        while shift < frame_count:
            lagged = jnp.pad(total, ((0, 0), (shift, 0)))[:, :-shift]
            total = total + power * lagged
            power = power * power
            shift *= 2
        return total

    slow_run = geometric_run(spikes, slow_col)
    fast_run = geometric_run(spikes, fast_col)
    kernel_scale = (1.0 - decay_slow) * (1.0 - decay_fast) / (decay_slow - decay_fast)
    return kernel_scale[:, None] * (slow_col * slow_run - fast_col * fast_run)


def tap_values():
    offsets = np.arange(-GR, GR + 1).astype(np.float64)
    raw = np.exp(-offsets * offsets / sigma_twice)
    taps = (raw / raw.sum()).astype(np.float32).astype(ml_dtypes.bfloat16)
    return taps.astype(np.float32)


def band_constants(col_count):
    index = np.arange(col_count)
    gap = index[None, :] - index[:, None]
    box = (np.abs(gap) <= RAD).astype(np.float32)
    side = (np.abs(gap) == RAD).astype(np.float32)
    taps = tap_values()
    blur = np.zeros((col_count, col_count), np.float32)
    for offset in range(-GR, GR + 1):
        blur = blur + np.where(gap == offset, taps[offset + GR], 0.0)
    wcat = np.concatenate([box, side], axis=0).astype(ml_dtypes.bfloat16)
    return wcat, blur.astype(ml_dtypes.bfloat16)


def stencil_kernel(edge_ref, top_ref, own_ref, bot_ref, wcat_ref, blur_ref, scale_ref, recip_ref,
                   frows_ref, back_ref, grad_ref, hsum_ref, ssum_ref, rows_ref, norm_ref):
    halo = top_ref.shape[0]
    own = own_ref.shape[0]
    cols = own_ref.shape[1]
    taps = [float(v) for v in tap_values()]

    def horizontal(e, row):
        prod = jnp.dot(wcat_ref[...], row, preferred_element_type=jnp.float32)
        hsum_ref[e] = prod[:cols]
        ssum_ref[e] = prod[cols:]

    def top_h(r, c):
        horizontal(r, top_ref[r])
        return c

    def own_h(r, c):
        horizontal(halo + r, own_ref[r])
        return c

    def bot_h(r, c):
        horizontal(halo + own + r, bot_ref[r])
        return c

    lax.fori_loop(0, halo, top_h, 0)
    lax.fori_loop(0, own, own_h, 0)
    lax.fori_loop(0, halo, bot_h, 0)

    first = halo - GR
    side = ssum_ref[first - RAD]
    for i in range(1, 2 * RAD - 1):
        side = side + ssum_ref[first - RAD + i]

    def detrend(k, side, row, keep):
        e = first + k
        side = side + ssum_ref[e + RAD - 1] - ssum_ref[e - RAD]
        total = hsum_ref[e - RAD] + hsum_ref[e + RAD] + side
        fit = scale_ref[...] * total
        residual_f = row.astype(jnp.float32)
        det = (residual_f - fit).astype(jnp.bfloat16)
        if keep is not None:
            det = (det.astype(jnp.float32) * keep).astype(jnp.bfloat16)
        rows_ref[k] = jnp.dot(blur_ref[...], det, preferred_element_type=jnp.float32)
        return side, fit

    keep_top = edge_ref[0]
    keep_bot = edge_ref[1]

    def top_d(k, side):
        side, _ = detrend(k, side, top_ref[first + k], keep_top)
        return side

    def own_d(r, side):
        side, fit = detrend(GR + r, side, own_ref[r], None)
        back_ref[r] = fit.astype(back_ref.dtype)
        return side

    def bot_d(r, side):
        side, _ = detrend(GR + own + r, side, bot_ref[r], keep_bot)
        return side

    side = lax.fori_loop(0, GR, top_d, side)
    side = lax.fori_loop(0, own, own_d, side)
    side = lax.fori_loop(0, GR, bot_d, side)

    def smooth(y, c):
        acc = taps[GR] * rows_ref[y + GR]
        for o in range(GR):
            acc = acc + taps[o] * (rows_ref[y + o] + rows_ref[y + 2 * GR - o])
        norm_ref[y] = (acc * recip_ref[y]).astype(jnp.bfloat16)
        return c

    lax.fori_loop(0, own, smooth, 0)
    frame_block = norm_ref.shape[2]
    grad_ref[...] = jnp.dot(
        frows_ref[...], norm_ref[...].reshape(own * cols, frame_block),
        preferred_element_type=jnp.float32,
    )


def stencil(edge, top, own, bot, scale, recip, frows, frame_block=128):
    halo, own_rows, cols, frames = top.shape[0], own.shape[0], own.shape[1], own.shape[2]
    slots = frows.shape[0]
    ext = 2 * halo + own_rows
    wcat, blur = band_constants(cols)
    grid = (frames // frame_block,)
    row_block = lambda n: pl.BlockSpec((n, cols, frame_block), lambda j: (0, 0, j))
    fixed = lambda shape: pl.BlockSpec(shape, lambda j: (0,) * len(shape))
    return pl.pallas_call(
        stencil_kernel,
        grid=grid,
        in_specs=[
            pl.BlockSpec(memory_space=pltpu.SMEM),
            row_block(halo), row_block(own_rows), row_block(halo),
            fixed((2 * cols, cols)), fixed((cols, cols)), fixed((cols, frame_block)),
            fixed((own_rows, cols, frame_block)), fixed((slots, own_rows * cols)),
        ],
        out_specs=[row_block(own_rows), pl.BlockSpec((slots, frame_block), lambda j: (0, j))],
        out_shape=[jax.ShapeDtypeStruct(own.shape, jnp.bfloat16),
                   jax.ShapeDtypeStruct((slots, frames), jnp.float32)],
        scratch_shapes=[
            pltpu.VMEM((ext, cols, frame_block), jnp.float32),
            pltpu.VMEM((ext, cols, frame_block), jnp.float32),
            pltpu.VMEM((own_rows + 2 * GR, cols, frame_block), jnp.float32),
            pltpu.VMEM((own_rows, cols, frame_block), jnp.bfloat16),
        ],
        compiler_params=pltpu.CompilerParams(vmem_limit_bytes=60 * 1024 * 1024),
    )(edge, top, own, bot, jnp.asarray(wcat), jnp.asarray(blur), scale, recip, frows)


MESH = pl.DeviceIdType.MESH


def exchange_kernel(out_ref, in_ref, mid_ref, first_send, first_recv, second_send, second_recv, local_sem):
    major, minor = out_ref.shape[0], out_ref.shape[1]
    me = lax.axis_index("pix")
    row, col = me // minor, me % minor
    barrier = pltpu.get_barrier_semaphore()

    def col_peer(k):
        return lax.rem(col + k, minor)

    def row_peer(k):
        return lax.rem(row + k, major)

    def first_copy(target_col, source_col):
        return pltpu.make_async_remote_copy(
            src_ref=out_ref.at[:, target_col],
            dst_ref=mid_ref.at[source_col],
            send_sem=first_send.at[target_col],
            recv_sem=first_recv.at[source_col],
            device_id={"pix": row * minor + target_col},
            device_id_type=MESH,
        )

    def second_copy(target_row, source_row):
        return pltpu.make_async_remote_copy(
            src_ref=mid_ref.at[:, target_row],
            dst_ref=in_ref.at[source_row],
            send_sem=second_send.at[target_row],
            recv_sem=second_recv.at[source_row],
            device_id={"pix": target_row * minor + col},
            device_id_type=MESH,
        )

    def greet_col(k, c):
        pl.semaphore_signal(barrier, inc=1, device_id={"pix": row * minor + col_peer(k)}, device_id_type=MESH)
        return c

    def greet_row(k, c):
        pl.semaphore_signal(barrier, inc=1, device_id={"pix": row_peer(k) * minor + col}, device_id_type=MESH)
        return c

    lax.fori_loop(1, minor, greet_col, 0)
    lax.fori_loop(1, major, greet_row, 0)
    pl.semaphore_wait(barrier, minor + major - 2)

    def launch_first(k, c):
        first_copy(col_peer(k), col).start()
        return c

    lax.fori_loop(1, minor, launch_first, 0)
    local = pltpu.make_async_copy(out_ref.at[:, col], mid_ref.at[col], local_sem)
    local.start()
    local.wait()

    def finish_first(k, c):
        first_copy(col_peer(k), col).wait_send()
        source = lax.rem(col + minor - k, minor)
        first_copy(source, source).wait_recv()
        return c

    lax.fori_loop(1, minor, finish_first, 0)

    def launch_second(k, c):
        second_copy(row_peer(k), row).start()
        return c

    lax.fori_loop(1, major, launch_second, 0)
    local = pltpu.make_async_copy(mid_ref.at[:, row], in_ref.at[row], local_sem)
    local.start()
    local.wait()

    def finish_second(k, c):
        second_copy(row_peer(k), row).wait_send()
        source = lax.rem(row + major - k, major)
        second_copy(source, source).wait_recv()
        return c

    lax.fori_loop(1, major, finish_second, 0)


def exchange(outbox, collective):
    count = outbox.shape[0]
    major = 4 if count % 4 == 0 and count > 4 else 1
    minor = count // major
    blocks = outbox.reshape((major, minor) + outbox.shape[1:])
    received, _ = pl.pallas_call(
        exchange_kernel,
        out_shape=[
            jax.ShapeDtypeStruct(blocks.shape, outbox.dtype),
            jax.ShapeDtypeStruct((minor, major) + outbox.shape[1:], outbox.dtype),
        ],
        in_specs=[pl.BlockSpec(memory_space=pl.ANY)],
        out_specs=[pl.BlockSpec(memory_space=pl.ANY), pl.BlockSpec(memory_space=pl.ANY)],
        scratch_shapes=[
            pltpu.SemaphoreType.DMA((minor,)),
            pltpu.SemaphoreType.DMA((minor,)),
            pltpu.SemaphoreType.DMA((major,)),
            pltpu.SemaphoreType.DMA((major,)),
            pltpu.SemaphoreType.DMA,
        ],
        compiler_params=pltpu.CompilerParams(collective_id=collective, has_side_effects=True),
    )(blocks)
    return received.reshape(outbox.shape)


def on_device(movie, footprints, traces, stripe, column, annulus_gain, decay_slow, decay_fast):
    pix_count = lax.axis_size("pix")
    row_count = movie.shape[1]
    col_count = movie.shape[2]
    frame_count = movie.shape[3]
    neuron_count = footprints.shape[1]
    capacity = max(2, 2 * neuron_count // pix_count)
    slot_count = pix_count * capacity
    target_stripe = stripe[0, :, 0]
    neuron_index = jnp.arange(neuron_count)
    earlier_same = (target_stripe[:, None] == target_stripe[None, :]) & (
        neuron_index[None, :] < neuron_index[:, None]
    )
    arrival_rank = jnp.sum(earlier_same.astype(jnp.int32), axis=1)
    slot_index = target_stripe * capacity + arrival_rank
    placement = slot_index[:, None] == jnp.arange(slot_count)[None, :]
    placement_b = placement.astype(jnp.bfloat16)
    contract_first = (((0,), (0,)), ((), ()))
    tile_width, trace_width = footprints.shape[2], traces.shape[2]
    column_lanes = jnp.broadcast_to(
        (column[0] + 1).astype(jnp.bfloat16)[:, None], (neuron_count, 128)
    )
    payload = jnp.concatenate([footprints[0], traces[0], column_lanes], axis=1)
    outbox = lax.dot_general(
        placement_b, payload, contract_first, preferred_element_type=jnp.float32
    ).astype(jnp.bfloat16)
    inbox = exchange(outbox.reshape(pix_count, capacity, -1), 0).reshape(slot_count, -1)
    tile_inbox = inbox[:, :tile_width]
    trace_inbox = inbox[:, tile_width : tile_width + trace_width]
    column_inbox = inbox[:, tile_width + trace_width].astype(jnp.int32)
    left_edge = column_inbox - 1
    covered = left_edge[:, None] + jnp.arange(FOOT)[None, :]
    column_onehot = (covered[:, :, None] == jnp.arange(col_count)[None, None, :]).astype(
        jnp.bfloat16
    )
    tile_grid = tile_inbox.reshape(slot_count, FOOT, FOOT)
    frows = jnp.einsum(
        "srj,sjc->src", tile_grid, column_onehot, preferred_element_type=jnp.float32
    ).astype(jnp.bfloat16)
    model_image = jnp.einsum(
        "src,st->rct", frows, trace_inbox, preferred_element_type=jnp.float32
    )
    residual = (movie[0].astype(jnp.float32) - model_image).astype(jnp.bfloat16)
    halo = RAD + GR
    pix_index = lax.axis_index("pix")
    up = [(i, i + 1) for i in range(pix_count - 1)]
    down = [(j, i) for i, j in up]
    top_halo = lax.ppermute(residual[row_count - halo :], "pix", up)
    bottom_halo = lax.ppermute(residual[:halo], "pix", down)
    frame_index = np.arange(frame_count)
    step_matrix = (
        (frame_index[:, None] == frame_index[None, :] + 1).astype(np.float32)
        - (frame_index[:, None] == frame_index[None, :]).astype(np.float32)
    ) * (frame_index[None, :] < frame_count - 1)
    frame_step = jnp.dot(
        residual.reshape(row_count * col_count, frame_count),
        jnp.asarray(step_matrix, jnp.bfloat16),
        preferred_element_type=jnp.float32,
    )
    noise_level = (jnp.sum(frame_step * frame_step, axis=1) / (frame_count - 1)).reshape(
        row_count, col_count
    )
    noise_stack = with_halo(noise_level[None], (("plane", 0),), 1)
    pooled = (noise_stack[0] + 2.0 * noise_stack[1] + noise_stack[2]) / 4.0
    frame_block = 128
    recip = jnp.broadcast_to(
        (1.0 / jnp.sqrt(pooled + noise_eps))[:, :, None], (row_count, col_count, frame_block)
    )
    scale = jnp.broadcast_to((annulus_gain[0] / (8.0 * RAD))[:, None], (col_count, frame_block))
    edge = jnp.stack([pix_index > 0, pix_index < pix_count - 1]).astype(jnp.float32)
    background, slot_gradient = stencil(
        edge, top_halo, residual, bottom_halo, scale, recip,
        frows.reshape(slot_count, row_count * col_count), frame_block
    )
    home_gradient = exchange(slot_gradient.reshape(pix_count, capacity, -1), 1).reshape(
        slot_count, -1
    )
    gradient = lax.dot_general(
        placement.astype(jnp.float32),
        home_gradient,
        (((1,), (0,)), ((), ())),
        precision=lax.Precision.HIGHEST,
    )
    foot_f = footprints[0].astype(jnp.float32)
    step_size = 1.0 / (jnp.sum(foot_f * foot_f, axis=1) + norm_eps)
    updated = traces[0].astype(jnp.float32) + step_size[:, None] * gradient
    spikes = deconvolve(updated, decay_slow[0], decay_fast[0])
    traces_new = reconvolve(spikes, decay_slow[0], decay_fast[0])
    return (background[None], traces_new[None])


def solution(mesh):
    placed = (
        P("plane", "pix", None, None),
        P("plane", "pix", None),
        P("plane", "pix", None),
        P("plane", "pix", None),
        P("plane", "pix"),
        P("plane", None),
        P("plane", "pix"),
        P("plane", "pix"),
    )
    return jax.shard_map(
        on_device,
        mesh=mesh,
        in_specs=placed,
        out_specs=(P("plane", "pix", None, None), P("plane", "pix", None)),
        check_vma=False,
    )
```

```python
import functools
import numpy as np
import ml_dtypes
import jax
import jax.numpy as jnp
from jax import lax
from jax.experimental import pallas as pl
from jax.experimental.pallas import tpu as pltpu
from jax.sharding import PartitionSpec as P

FOOT = 32
RAD = 12
GR = 3


lam_floor = 0.1
noise_eps = 1e-05
norm_eps = 1e-05
sigma_twice = 4.5


def with_halo(array, sides, width):
    for axis, dim in sides:
        devices, length = (lax.axis_size(axis), array.shape[dim])
        up = [(i, (i + 1) % devices) for i in range(devices - 1)]
        down = [(j, i) for i, j in up]
        last = lax.slice_in_dim(array, length - width, length, axis=dim)
        initial = lax.slice_in_dim(array, 0, width, axis=dim)
        before = lax.ppermute(last, axis, up)
        after = lax.ppermute(initial, axis, down)
        array = jnp.concatenate([before, array, after], axis=dim)
    return array


def deconvolve(updated, decay_slow, decay_fast):
    lag_one = jnp.pad(updated, ((0, 0), (1, 0)))[:, :-1]
    lag_two = jnp.pad(updated, ((0, 0), (2, 0)))[:, :-2]
    driven = (
        updated
        - (decay_slow + decay_fast)[:, None] * lag_one
        + (decay_slow * decay_fast)[:, None] * lag_two
    )
    return jnp.maximum(driven - lam_floor, 0.0)


def reconvolve(spikes, decay_slow, decay_fast):
    frame_count = spikes.shape[1]
    slow_col, fast_col = decay_slow[:, None], decay_fast[:, None]

    def geometric_run(values, ratio):
        total, power, shift = values, ratio, 1
        while shift < frame_count:
            lagged = jnp.pad(total, ((0, 0), (shift, 0)))[:, :-shift]
            total = total + power * lagged
            power = power * power
            shift *= 2
        return total

    slow_run = geometric_run(spikes, slow_col)
    fast_run = geometric_run(spikes, fast_col)
    kernel_scale = (1.0 - decay_slow) * (1.0 - decay_fast) / (decay_slow - decay_fast)
    return kernel_scale[:, None] * (slow_col * slow_run - fast_col * fast_run)


def tap_values():
    offsets = np.arange(-GR, GR + 1).astype(np.float64)
    raw = np.exp(-offsets * offsets / sigma_twice)
    taps = (raw / raw.sum()).astype(np.float32).astype(ml_dtypes.bfloat16)
    return taps.astype(np.float32)


def band_constants(col_count):
    index = np.arange(col_count)
    gap = index[None, :] - index[:, None]
    box = (np.abs(gap) <= RAD).astype(np.float32)
    side = (np.abs(gap) == RAD).astype(np.float32)
    taps = tap_values()
    blur = np.zeros((col_count, col_count), np.float32)
    for offset in range(-GR, GR + 1):
        blur = blur + np.where(gap == offset, taps[offset + GR], 0.0)
    wcat = np.concatenate([box, side], axis=0).astype(ml_dtypes.bfloat16)
    return wcat, blur.astype(ml_dtypes.bfloat16)


def stencil_kernel(edge_ref, top_ref, own_ref, bot_ref, wcat_ref, blur_ref, scale_ref, recip_ref,
                   frows_ref, back_ref, grad_ref, hsum_ref, ssum_ref, rows_ref, norm_ref):
    halo = top_ref.shape[0]
    own = own_ref.shape[0]
    cols = own_ref.shape[1]
    taps = [float(v) for v in tap_values()]

    def horizontal(e, row):
        prod = jnp.dot(wcat_ref[...], row, preferred_element_type=jnp.float32)
        hsum_ref[e] = prod[:cols]
        ssum_ref[e] = prod[cols:]

    def top_h(r, c):
        horizontal(r, top_ref[r])
        return c

    def own_h(r, c):
        horizontal(halo + r, own_ref[r])
        return c

    def bot_h(r, c):
        horizontal(halo + own + r, bot_ref[r])
        return c

    lax.fori_loop(0, halo, top_h, 0)
    lax.fori_loop(0, own, own_h, 0)
    lax.fori_loop(0, halo, bot_h, 0)

    first = halo - GR
    side = ssum_ref[first - RAD]
    for i in range(1, 2 * RAD - 1):
        side = side + ssum_ref[first - RAD + i]

    def detrend(k, side, row, keep):
        e = first + k
        side = side + ssum_ref[e + RAD - 1] - ssum_ref[e - RAD]
        total = hsum_ref[e - RAD] + hsum_ref[e + RAD] + side
        fit = scale_ref[...] * total
        residual_f = row.astype(jnp.float32)
        det = (residual_f - fit).astype(jnp.bfloat16)
        if keep is not None:
            det = (det.astype(jnp.float32) * keep).astype(jnp.bfloat16)
        rows_ref[k] = jnp.dot(blur_ref[...], det, preferred_element_type=jnp.float32)
        return side, fit

    keep_top = edge_ref[0]
    keep_bot = edge_ref[1]

    def top_d(k, side):
        side, _ = detrend(k, side, top_ref[first + k], keep_top)
        return side

    def own_d(r, side):
        side, fit = detrend(GR + r, side, own_ref[r], None)
        back_ref[r] = fit.astype(back_ref.dtype)
        return side

    def bot_d(r, side):
        side, _ = detrend(GR + own + r, side, bot_ref[r], keep_bot)
        return side

    side = lax.fori_loop(0, GR, top_d, side)
    side = lax.fori_loop(0, own, own_d, side)
    side = lax.fori_loop(0, GR, bot_d, side)

    def smooth(y, c):
        acc = taps[GR] * rows_ref[y + GR]
        for o in range(GR):
            acc = acc + taps[o] * (rows_ref[y + o] + rows_ref[y + 2 * GR - o])
        norm_ref[y] = (acc * recip_ref[y]).astype(jnp.bfloat16)
        return c

    lax.fori_loop(0, own, smooth, 0)
    frame_block = norm_ref.shape[2]
    grad_ref[...] = jnp.dot(
        frows_ref[...], norm_ref[...].reshape(own * cols, frame_block),
        preferred_element_type=jnp.float32,
    )


def stencil(edge, top, own, bot, scale, recip, frows, frame_block=128):
    halo, own_rows, cols, frames = top.shape[0], own.shape[0], own.shape[1], own.shape[2]
    slots = frows.shape[0]
    ext = 2 * halo + own_rows
    wcat, blur = band_constants(cols)
    grid = (frames // frame_block,)
    row_block = lambda n: pl.BlockSpec((n, cols, frame_block), lambda j: (0, 0, j))
    fixed = lambda shape: pl.BlockSpec(shape, lambda j: (0,) * len(shape))
    return pl.pallas_call(
        stencil_kernel,
        grid=grid,
        in_specs=[
            pl.BlockSpec(memory_space=pltpu.SMEM),
            row_block(halo), row_block(own_rows), row_block(halo),
            fixed((2 * cols, cols)), fixed((cols, cols)), fixed((cols, frame_block)),
            fixed((own_rows, cols, frame_block)), fixed((slots, own_rows * cols)),
        ],
        out_specs=[row_block(own_rows), pl.BlockSpec((slots, frame_block), lambda j: (0, j))],
        out_shape=[jax.ShapeDtypeStruct(own.shape, jnp.bfloat16),
                   jax.ShapeDtypeStruct((slots, frames), jnp.float32)],
        scratch_shapes=[
            pltpu.VMEM((ext, cols, frame_block), jnp.float32),
            pltpu.VMEM((ext, cols, frame_block), jnp.float32),
            pltpu.VMEM((own_rows + 2 * GR, cols, frame_block), jnp.float32),
            pltpu.VMEM((own_rows, cols, frame_block), jnp.bfloat16),
        ],
        compiler_params=pltpu.CompilerParams(vmem_limit_bytes=60 * 1024 * 1024),
    )(edge, top, own, bot, jnp.asarray(wcat), jnp.asarray(blur), scale, recip, frows)


MESH = pl.DeviceIdType.MESH


def exchange_kernel(out_ref, in_ref, send_sem, recv_sem, local_sem):
    count = out_ref.shape[0]
    me = lax.axis_index("pix")
    barrier = pltpu.get_barrier_semaphore()

    def peer_at(k):
        return lax.rem(me + k, count)

    def source_at(k):
        return lax.rem(me + count - k, count)

    def remote(target, block):
        return pltpu.make_async_remote_copy(
            src_ref=out_ref.at[target],
            dst_ref=in_ref.at[block],
            send_sem=send_sem.at[target],
            recv_sem=recv_sem.at[block],
            device_id={"pix": target},
            device_id_type=MESH,
        )

    def greet(k, c):
        pl.semaphore_signal(barrier, inc=1, device_id={"pix": peer_at(k)}, device_id_type=MESH)
        return c

    lax.fori_loop(1, count, greet, 0)
    pl.semaphore_wait(barrier, count - 1)

    def launch(k, c):
        remote(peer_at(k), me).start()
        return c

    lax.fori_loop(1, count, launch, 0)
    local = pltpu.make_async_copy(out_ref.at[me], in_ref.at[me], local_sem)
    local.start()
    local.wait()

    def finish(k, c):
        remote(peer_at(k), me).wait_send()
        remote(source_at(k), source_at(k)).wait_recv()
        return c

    lax.fori_loop(1, count, finish, 0)


def exchange(outbox, collective):
    count = outbox.shape[0]
    return pl.pallas_call(
        exchange_kernel,
        out_shape=jax.ShapeDtypeStruct(outbox.shape, outbox.dtype),
        in_specs=[pl.BlockSpec(memory_space=pl.ANY)],
        out_specs=pl.BlockSpec(memory_space=pl.ANY),
        scratch_shapes=[
            pltpu.SemaphoreType.DMA((count,)),
            pltpu.SemaphoreType.DMA((count,)),
            pltpu.SemaphoreType.DMA,
        ],
        compiler_params=pltpu.CompilerParams(collective_id=collective, has_side_effects=True),
    )(outbox)


def on_device(movie, footprints, traces, stripe, column, annulus_gain, decay_slow, decay_fast):
    pix_count = lax.axis_size("pix")
    row_count = movie.shape[1]
    col_count = movie.shape[2]
    frame_count = movie.shape[3]
    neuron_count = footprints.shape[1]
    capacity = max(2, 2 * neuron_count // pix_count)
    slot_count = pix_count * capacity
    target_stripe = stripe[0, :, 0]
    neuron_index = jnp.arange(neuron_count)
    earlier_same = (target_stripe[:, None] == target_stripe[None, :]) & (
        neuron_index[None, :] < neuron_index[:, None]
    )
    arrival_rank = jnp.sum(earlier_same.astype(jnp.int32), axis=1)
    slot_index = target_stripe * capacity + arrival_rank
    placement = slot_index[:, None] == jnp.arange(slot_count)[None, :]
    placement_b = placement.astype(jnp.bfloat16)
    contract_first = (((0,), (0,)), ((), ()))
    tile_width, trace_width = footprints.shape[2], traces.shape[2]
    column_lanes = jnp.broadcast_to(
        (column[0] + 1).astype(jnp.bfloat16)[:, None], (neuron_count, 128)
    )
    payload = jnp.concatenate([footprints[0], traces[0], column_lanes], axis=1)
    outbox = lax.dot_general(
        placement_b, payload, contract_first, preferred_element_type=jnp.float32
    ).astype(jnp.bfloat16)
    inbox = exchange(outbox.reshape(pix_count, capacity, -1), 0).reshape(slot_count, -1)
    tile_inbox = inbox[:, :tile_width]
    trace_inbox = inbox[:, tile_width : tile_width + trace_width]
    column_inbox = inbox[:, tile_width + trace_width].astype(jnp.int32)
    left_edge = column_inbox - 1
    covered = left_edge[:, None] + jnp.arange(FOOT)[None, :]
    column_onehot = (covered[:, :, None] == jnp.arange(col_count)[None, None, :]).astype(
        jnp.bfloat16
    )
    tile_grid = tile_inbox.reshape(slot_count, FOOT, FOOT)
    frows = jnp.einsum(
        "srj,sjc->src", tile_grid, column_onehot, preferred_element_type=jnp.float32
    ).astype(jnp.bfloat16)
    frows_t = jnp.einsum(
        "srj,sjc->rcs", tile_grid, column_onehot, preferred_element_type=jnp.float32
    ).astype(jnp.bfloat16)
    model_image = jnp.einsum(
        "rcs,st->rct", frows_t, trace_inbox, preferred_element_type=jnp.float32
    )
    residual = (movie[0].astype(jnp.float32) - model_image).astype(jnp.bfloat16)
    halo = RAD + GR
    pix_index = lax.axis_index("pix")
    up = [(i, i + 1) for i in range(pix_count - 1)]
    down = [(j, i) for i, j in up]
    top_halo = lax.ppermute(residual[row_count - halo :], "pix", up)
    bottom_halo = lax.ppermute(residual[:halo], "pix", down)
    frame_index = np.arange(frame_count)
    step_matrix = (
        (frame_index[:, None] == frame_index[None, :] + 1).astype(np.float32)
        - (frame_index[:, None] == frame_index[None, :]).astype(np.float32)
    ) * (frame_index[None, :] < frame_count - 1)
    frame_step = jnp.dot(
        residual.reshape(row_count * col_count, frame_count),
        jnp.asarray(step_matrix, jnp.bfloat16),
        preferred_element_type=jnp.float32,
    )
    noise_level = (jnp.sum(frame_step * frame_step, axis=1) / (frame_count - 1)).reshape(
        row_count, col_count
    )
    noise_stack = with_halo(noise_level[None], (("plane", 0),), 1)
    pooled = (noise_stack[0] + 2.0 * noise_stack[1] + noise_stack[2]) / 4.0
    frame_block = 128
    recip = jnp.broadcast_to(
        (1.0 / jnp.sqrt(pooled + noise_eps))[:, :, None], (row_count, col_count, frame_block)
    )
    scale = jnp.broadcast_to((annulus_gain[0] / (8.0 * RAD))[:, None], (col_count, frame_block))
    edge = jnp.stack([pix_index > 0, pix_index < pix_count - 1]).astype(jnp.float32)
    background, slot_gradient = stencil(
        edge, top_halo, residual, bottom_halo, scale, recip,
        frows.reshape(slot_count, row_count * col_count), frame_block
    )
    home_gradient = exchange(slot_gradient.reshape(pix_count, capacity, -1), 1).reshape(
        slot_count, -1
    )
    gradient = lax.dot_general(
        placement.astype(jnp.float32),
        home_gradient,
        (((1,), (0,)), ((), ())),
        precision=lax.Precision.HIGHEST,
    )
    foot_f = footprints[0].astype(jnp.float32)
    step_size = 1.0 / (jnp.sum(foot_f * foot_f, axis=1) + norm_eps)
    updated = traces[0].astype(jnp.float32) + step_size[:, None] * gradient
    spikes = deconvolve(updated, decay_slow[0], decay_fast[0])
    traces_new = reconvolve(spikes, decay_slow[0], decay_fast[0])
    return (background[None], traces_new[None])


def solution(mesh):
    placed = (
        P("plane", "pix", None, None),
        P("plane", "pix", None),
        P("plane", "pix", None),
        P("plane", "pix", None),
        P("plane", "pix"),
        P("plane", None),
        P("plane", "pix"),
        P("plane", "pix"),
    )
    return jax.shard_map(
        on_device,
        mesh=mesh,
        in_specs=placed,
        out_specs=(P("plane", "pix", None, None), P("plane", "pix", None)),
        check_vma=False,
    )
```

```python
import functools
import numpy as np
import ml_dtypes
import jax
import jax.numpy as jnp
from jax import lax
from jax.experimental import pallas as pl
from jax.experimental.pallas import tpu as pltpu
from jax.sharding import PartitionSpec as P

FOOT = 32
RAD = 12
GR = 3


lam_floor = 0.1
noise_eps = 1e-05
norm_eps = 1e-05
sigma_twice = 4.5


def with_halo(array, sides, width):
    for axis, dim in sides:
        devices, length = (lax.axis_size(axis), array.shape[dim])
        up = [(i, (i + 1) % devices) for i in range(devices - 1)]
        down = [(j, i) for i, j in up]
        last = lax.slice_in_dim(array, length - width, length, axis=dim)
        initial = lax.slice_in_dim(array, 0, width, axis=dim)
        before = lax.ppermute(last, axis, up)
        after = lax.ppermute(initial, axis, down)
        array = jnp.concatenate([before, array, after], axis=dim)
    return array


def deconvolve(updated, decay_slow, decay_fast):
    lag_one = jnp.pad(updated, ((0, 0), (1, 0)))[:, :-1]
    lag_two = jnp.pad(updated, ((0, 0), (2, 0)))[:, :-2]
    driven = (
        updated
        - (decay_slow + decay_fast)[:, None] * lag_one
        + (decay_slow * decay_fast)[:, None] * lag_two
    )
    return jnp.maximum(driven - lam_floor, 0.0)


def reconvolve(spikes, decay_slow, decay_fast):
    frame_count = spikes.shape[1]
    slow_col, fast_col = decay_slow[:, None], decay_fast[:, None]

    def geometric_run(values, ratio):
        total, power, shift = values, ratio, 1
        while shift < frame_count:
            lagged = jnp.pad(total, ((0, 0), (shift, 0)))[:, :-shift]
            total = total + power * lagged
            power = power * power
            shift *= 2
        return total

    slow_run = geometric_run(spikes, slow_col)
    fast_run = geometric_run(spikes, fast_col)
    kernel_scale = (1.0 - decay_slow) * (1.0 - decay_fast) / (decay_slow - decay_fast)
    return kernel_scale[:, None] * (slow_col * slow_run - fast_col * fast_run)


def tap_values():
    offsets = np.arange(-GR, GR + 1).astype(np.float64)
    raw = np.exp(-offsets * offsets / sigma_twice)
    taps = (raw / raw.sum()).astype(np.float32).astype(ml_dtypes.bfloat16)
    return taps.astype(np.float32)


def band_constants(col_count):
    index = np.arange(col_count)
    gap = index[None, :] - index[:, None]
    box = (np.abs(gap) <= RAD).astype(np.float32)
    side = (np.abs(gap) == RAD).astype(np.float32)
    taps = tap_values()
    blur = np.zeros((col_count, col_count), np.float32)
    for offset in range(-GR, GR + 1):
        blur = blur + np.where(gap == offset, taps[offset + GR], 0.0)
    wcat = np.concatenate([box, side], axis=0).astype(ml_dtypes.bfloat16)
    return wcat, blur.astype(ml_dtypes.bfloat16)


def stencil_kernel(edge_ref, top_ref, own_ref, bot_ref, wcat_ref, blur_ref, scale_ref, recip_ref,
                   frows_ref, back_ref, grad_ref, hsum_ref, ssum_ref, rows_ref, norm_ref):
    halo = top_ref.shape[0]
    own = own_ref.shape[0]
    cols = own_ref.shape[1]
    taps = [float(v) for v in tap_values()]

    def horizontal(e, row):
        prod = jnp.dot(wcat_ref[...], row, preferred_element_type=jnp.float32)
        hsum_ref[e] = prod[:cols]
        ssum_ref[e] = prod[cols:]

    def top_h(r, c):
        horizontal(r, top_ref[r])
        return c

    def own_h(r, c):
        horizontal(halo + r, own_ref[r])
        return c

    def bot_h(r, c):
        horizontal(halo + own + r, bot_ref[r])
        return c

    lax.fori_loop(0, halo, top_h, 0)
    lax.fori_loop(0, own, own_h, 0)
    lax.fori_loop(0, halo, bot_h, 0)

    first = halo - GR
    side = ssum_ref[first - RAD]
    for i in range(1, 2 * RAD - 1):
        side = side + ssum_ref[first - RAD + i]

    def detrend(k, side, row, keep):
        e = first + k
        side = side + ssum_ref[e + RAD - 1] - ssum_ref[e - RAD]
        total = hsum_ref[e - RAD] + hsum_ref[e + RAD] + side
        fit = scale_ref[...] * total
        residual_f = row.astype(jnp.float32)
        det = (residual_f - fit).astype(jnp.bfloat16)
        if keep is not None:
            det = (det.astype(jnp.float32) * keep).astype(jnp.bfloat16)
        rows_ref[k] = jnp.dot(blur_ref[...], det, preferred_element_type=jnp.float32)
        return side, fit

    keep_top = edge_ref[0]
    keep_bot = edge_ref[1]

    def top_d(k, side):
        side, _ = detrend(k, side, top_ref[first + k], keep_top)
        return side

    def own_d(r, side):
        side, fit = detrend(GR + r, side, own_ref[r], None)
        back_ref[r] = fit.astype(back_ref.dtype)
        return side

    def bot_d(r, side):
        side, _ = detrend(GR + own + r, side, bot_ref[r], keep_bot)
        return side

    side = lax.fori_loop(0, GR, top_d, side)
    side = lax.fori_loop(0, own, own_d, side)
    side = lax.fori_loop(0, GR, bot_d, side)

    def smooth(y, c):
        acc = taps[GR] * rows_ref[y + GR]
        for o in range(GR):
            acc = acc + taps[o] * (rows_ref[y + o] + rows_ref[y + 2 * GR - o])
        norm_ref[y] = (acc * recip_ref[y]).astype(jnp.bfloat16)
        return c

    lax.fori_loop(0, own, smooth, 0)
    frame_block = norm_ref.shape[2]
    grad_ref[...] = jnp.dot(
        frows_ref[...], norm_ref[...].reshape(own * cols, frame_block),
        preferred_element_type=jnp.float32,
    )


def stencil(edge, top, own, bot, scale, recip, frows, frame_block=128):
    halo, own_rows, cols, frames = top.shape[0], own.shape[0], own.shape[1], own.shape[2]
    slots = frows.shape[0]
    ext = 2 * halo + own_rows
    wcat, blur = band_constants(cols)
    grid = (frames // frame_block,)
    row_block = lambda n: pl.BlockSpec((n, cols, frame_block), lambda j: (0, 0, j))
    fixed = lambda shape: pl.BlockSpec(shape, lambda j: (0,) * len(shape))
    return pl.pallas_call(
        stencil_kernel,
        grid=grid,
        in_specs=[
            pl.BlockSpec(memory_space=pltpu.SMEM),
            row_block(halo), row_block(own_rows), row_block(halo),
            fixed((2 * cols, cols)), fixed((cols, cols)), fixed((cols, frame_block)),
            fixed((own_rows, cols, frame_block)), fixed((slots, own_rows * cols)),
        ],
        out_specs=[row_block(own_rows), pl.BlockSpec((slots, frame_block), lambda j: (0, j))],
        out_shape=[jax.ShapeDtypeStruct(own.shape, jnp.bfloat16),
                   jax.ShapeDtypeStruct((slots, frames), jnp.float32)],
        scratch_shapes=[
            pltpu.VMEM((ext, cols, frame_block), jnp.float32),
            pltpu.VMEM((ext, cols, frame_block), jnp.float32),
            pltpu.VMEM((own_rows + 2 * GR, cols, frame_block), jnp.float32),
            pltpu.VMEM((own_rows, cols, frame_block), jnp.bfloat16),
        ],
        compiler_params=pltpu.CompilerParams(vmem_limit_bytes=60 * 1024 * 1024),
    )(edge, top, own, bot, jnp.asarray(wcat), jnp.asarray(blur), scale, recip, frows)


MESH = pl.DeviceIdType.MESH


def exchange_kernel(out_ref, in_ref, send_sem, recv_sem, local_sem):
    count = out_ref.shape[0]
    me = lax.axis_index("pix")
    barrier = pltpu.get_barrier_semaphore()

    def peer_at(k):
        return lax.rem(me + k, count)

    def source_at(k):
        return lax.rem(me + count - k, count)

    def remote(target, block):
        return pltpu.make_async_remote_copy(
            src_ref=out_ref.at[target],
            dst_ref=in_ref.at[block],
            send_sem=send_sem.at[target],
            recv_sem=recv_sem.at[block],
            device_id={"pix": target},
            device_id_type=MESH,
        )

    def greet(k, c):
        pl.semaphore_signal(barrier, inc=1, device_id={"pix": peer_at(k)}, device_id_type=MESH)
        return c

    lax.fori_loop(1, count, greet, 0)
    pl.semaphore_wait(barrier, count - 1)

    def launch(k, c):
        remote(peer_at(k), me).start()
        return c

    lax.fori_loop(1, count, launch, 0)
    local = pltpu.make_async_copy(out_ref.at[me], in_ref.at[me], local_sem)
    local.start()
    local.wait()

    def finish(k, c):
        remote(peer_at(k), me).wait_send()
        remote(source_at(k), source_at(k)).wait_recv()
        return c

    lax.fori_loop(1, count, finish, 0)


def exchange(outbox, collective):
    count = outbox.shape[0]
    return pl.pallas_call(
        exchange_kernel,
        out_shape=jax.ShapeDtypeStruct(outbox.shape, outbox.dtype),
        in_specs=[pl.BlockSpec(memory_space=pl.ANY)],
        out_specs=pl.BlockSpec(memory_space=pl.ANY),
        scratch_shapes=[
            pltpu.SemaphoreType.DMA((count,)),
            pltpu.SemaphoreType.DMA((count,)),
            pltpu.SemaphoreType.DMA,
        ],
        compiler_params=pltpu.CompilerParams(collective_id=collective, has_side_effects=True),
    )(outbox)


def on_device(movie, footprints, traces, stripe, column, annulus_gain, decay_slow, decay_fast):
    pix_count = lax.axis_size("pix")
    row_count = movie.shape[1]
    col_count = movie.shape[2]
    frame_count = movie.shape[3]
    neuron_count = footprints.shape[1]
    capacity = max(2, 2 * neuron_count // pix_count)
    slot_count = pix_count * capacity
    target_stripe = stripe[0, :, 0]
    neuron_index = jnp.arange(neuron_count)
    earlier_same = (target_stripe[:, None] == target_stripe[None, :]) & (
        neuron_index[None, :] < neuron_index[:, None]
    )
    arrival_rank = jnp.sum(earlier_same.astype(jnp.int32), axis=1)
    slot_index = target_stripe * capacity + arrival_rank
    placement = slot_index[:, None] == jnp.arange(slot_count)[None, :]
    placement_b = placement.astype(jnp.bfloat16)
    contract_first = (((0,), (0,)), ((), ()))
    tile_width, trace_width = footprints.shape[2], traces.shape[2]
    column_lanes = jnp.broadcast_to(
        (column[0] + 1).astype(jnp.bfloat16)[:, None], (neuron_count, 128)
    )
    payload = jnp.concatenate([footprints[0], traces[0], column_lanes], axis=1)
    outbox = lax.dot_general(
        placement_b, payload, contract_first, preferred_element_type=jnp.float32
    ).astype(jnp.bfloat16)
    inbox = exchange(outbox.reshape(pix_count, capacity, -1), 0).reshape(slot_count, -1)
    tile_inbox = inbox[:, :tile_width]
    trace_inbox = inbox[:, tile_width : tile_width + trace_width]
    column_inbox = inbox[:, tile_width + trace_width].astype(jnp.int32)
    left_edge = column_inbox - 1
    covered = left_edge[:, None] + jnp.arange(FOOT)[None, :]
    column_onehot = (covered[:, :, None] == jnp.arange(col_count)[None, None, :]).astype(
        jnp.bfloat16
    )
    tile_grid = tile_inbox.reshape(slot_count, FOOT, FOOT)
    frows = jnp.einsum(
        "srj,sjc->src", tile_grid, column_onehot, preferred_element_type=jnp.float32
    ).astype(jnp.bfloat16)
    frows_t = jnp.einsum(
        "srj,sjc->rcs", tile_grid, column_onehot, preferred_element_type=jnp.float32
    ).astype(jnp.bfloat16)
    model_image = jnp.einsum(
        "rcs,st->rct", frows_t, trace_inbox, preferred_element_type=jnp.float32
    )
    residual = (movie[0].astype(jnp.float32) - model_image).astype(jnp.bfloat16)
    halo = RAD + GR
    pix_index = lax.axis_index("pix")
    up = [(i, i + 1) for i in range(pix_count - 1)]
    down = [(j, i) for i, j in up]
    def edge_rows(first, count):
        model_rows = jnp.einsum(
            "rcs,st->rct", frows_t[first : first + count], trace_inbox,
            preferred_element_type=jnp.float32,
        )
        movie_rows = movie[0, first : first + count].astype(jnp.float32)
        return (movie_rows - model_rows).astype(jnp.bfloat16)

    top_halo = lax.ppermute(edge_rows(row_count - halo, halo), "pix", up)
    bottom_halo = lax.ppermute(edge_rows(0, halo), "pix", down)
    frame_index = np.arange(frame_count)
    step_matrix = (
        (frame_index[:, None] == frame_index[None, :] + 1).astype(np.float32)
        - (frame_index[:, None] == frame_index[None, :]).astype(np.float32)
    ) * (frame_index[None, :] < frame_count - 1)
    frame_step = jnp.dot(
        residual.reshape(row_count * col_count, frame_count),
        jnp.asarray(step_matrix, jnp.bfloat16),
        preferred_element_type=jnp.float32,
    )
    noise_level = (jnp.sum(frame_step * frame_step, axis=1) / (frame_count - 1)).reshape(
        row_count, col_count
    )
    noise_stack = with_halo(noise_level[None], (("plane", 0),), 1)
    pooled = (noise_stack[0] + 2.0 * noise_stack[1] + noise_stack[2]) / 4.0
    frame_block = 128
    recip = jnp.broadcast_to(
        (1.0 / jnp.sqrt(pooled + noise_eps))[:, :, None], (row_count, col_count, frame_block)
    )
    scale = jnp.broadcast_to((annulus_gain[0] / (8.0 * RAD))[:, None], (col_count, frame_block))
    edge = jnp.stack([pix_index > 0, pix_index < pix_count - 1]).astype(jnp.float32)
    background, slot_gradient = stencil(
        edge, top_halo, residual, bottom_halo, scale, recip,
        frows.reshape(slot_count, row_count * col_count), frame_block
    )
    home_gradient = exchange(slot_gradient.reshape(pix_count, capacity, -1), 1).reshape(
        slot_count, -1
    )
    gradient = lax.dot_general(
        placement.astype(jnp.float32),
        home_gradient,
        (((1,), (0,)), ((), ())),
        precision=lax.Precision.HIGHEST,
    )
    foot_f = footprints[0].astype(jnp.float32)
    step_size = 1.0 / (jnp.sum(foot_f * foot_f, axis=1) + norm_eps)
    updated = traces[0].astype(jnp.float32) + step_size[:, None] * gradient
    spikes = deconvolve(updated, decay_slow[0], decay_fast[0])
    traces_new = reconvolve(spikes, decay_slow[0], decay_fast[0])
    return (background[None], traces_new[None])


def solution(mesh):
    placed = (
        P("plane", "pix", None, None),
        P("plane", "pix", None),
        P("plane", "pix", None),
        P("plane", "pix", None),
        P("plane", "pix"),
        P("plane", None),
        P("plane", "pix"),
        P("plane", "pix"),
    )
    return jax.shard_map(
        on_device,
        mesh=mesh,
        in_specs=placed,
        out_specs=(P("plane", "pix", None, None), P("plane", "pix", None)),
        check_vma=False,
    )
```

```python
import functools
import numpy as np
import ml_dtypes
import jax
import jax.numpy as jnp
from jax import lax
from jax.experimental import pallas as pl
from jax.experimental.pallas import tpu as pltpu
from jax.sharding import PartitionSpec as P

FOOT = 32
RAD = 12
GR = 3


lam_floor = 0.1
noise_eps = 1e-05
norm_eps = 1e-05
sigma_twice = 4.5


def with_halo(array, sides, width):
    for axis, dim in sides:
        devices, length = (lax.axis_size(axis), array.shape[dim])
        up = [(i, (i + 1) % devices) for i in range(devices - 1)]
        down = [(j, i) for i, j in up]
        last = lax.slice_in_dim(array, length - width, length, axis=dim)
        initial = lax.slice_in_dim(array, 0, width, axis=dim)
        before = lax.ppermute(last, axis, up)
        after = lax.ppermute(initial, axis, down)
        array = jnp.concatenate([before, array, after], axis=dim)
    return array


def deconvolve(updated, decay_slow, decay_fast):
    lag_one = jnp.pad(updated, ((0, 0), (1, 0)))[:, :-1]
    lag_two = jnp.pad(updated, ((0, 0), (2, 0)))[:, :-2]
    driven = (
        updated
        - (decay_slow + decay_fast)[:, None] * lag_one
        + (decay_slow * decay_fast)[:, None] * lag_two
    )
    return jnp.maximum(driven - lam_floor, 0.0)


def reconvolve(spikes, decay_slow, decay_fast):
    frame_count = spikes.shape[1]
    slow_col, fast_col = decay_slow[:, None], decay_fast[:, None]

    def geometric_run(values, ratio):
        total, power, shift = values, ratio, 1
        while shift < frame_count:
            lagged = jnp.pad(total, ((0, 0), (shift, 0)))[:, :-shift]
            total = total + power * lagged
            power = power * power
            shift *= 2
        return total

    slow_run = geometric_run(spikes, slow_col)
    fast_run = geometric_run(spikes, fast_col)
    kernel_scale = (1.0 - decay_slow) * (1.0 - decay_fast) / (decay_slow - decay_fast)
    return kernel_scale[:, None] * (slow_col * slow_run - fast_col * fast_run)


def tap_values():
    offsets = np.arange(-GR, GR + 1).astype(np.float64)
    raw = np.exp(-offsets * offsets / sigma_twice)
    taps = (raw / raw.sum()).astype(np.float32).astype(ml_dtypes.bfloat16)
    return taps.astype(np.float32)


def band_constants(col_count):
    index = np.arange(col_count)
    gap = index[None, :] - index[:, None]
    box = (np.abs(gap) <= RAD).astype(np.float32)
    side = (np.abs(gap) == RAD).astype(np.float32)
    taps = tap_values()
    blur = np.zeros((col_count, col_count), np.float32)
    for offset in range(-GR, GR + 1):
        blur = blur + np.where(gap == offset, taps[offset + GR], 0.0)
    as_bf16 = lambda x: x.astype(ml_dtypes.bfloat16)
    pair = np.concatenate([box, box], axis=1)
    slide = np.concatenate([side, -side], axis=1)
    return as_bf16(pair), as_bf16(slide), as_bf16(side), as_bf16(blur)


def stencil_kernel(edge_ref, top_ref, own_ref, bot_ref, pair_ref, slide_ref, side_ref, blur_ref,
                   scale_ref, recip_ref, frows_ref, back_ref, grad_ref, ext_ref, rows_ref, norm_ref):
    halo = top_ref.shape[0]
    own = own_ref.shape[0]
    taps = [float(v) for v in tap_values()]

    def copy_top(r, c):
        ext_ref[r] = top_ref[r]
        return c

    def copy_own(r, c):
        ext_ref[halo + r] = own_ref[r]
        return c

    def copy_bot(r, c):
        ext_ref[halo + own + r] = bot_ref[r]
        return c

    lax.fori_loop(0, halo, copy_top, 0)
    lax.fori_loop(0, own, copy_own, 0)
    lax.fori_loop(0, halo, copy_bot, 0)

    first = halo - GR
    side = jnp.dot(side_ref[...], ext_ref[first - RAD], preferred_element_type=jnp.float32)
    for i in range(1, 2 * RAD - 1):
        side = side + jnp.dot(
            side_ref[...], ext_ref[first - RAD + i], preferred_element_type=jnp.float32
        )

    def detrend(k, side, keep):
        e = first + k
        above, below = ext_ref[e - RAD], ext_ref[e + RAD]
        step = jnp.dot(
            slide_ref[...], jnp.concatenate([ext_ref[e + RAD - 1], above], axis=0),
            preferred_element_type=jnp.float32,
        )
        side = side + step
        ring = jnp.dot(
            pair_ref[...], jnp.concatenate([above, below], axis=0),
            preferred_element_type=jnp.float32,
        )
        total = ring + side
        fit = scale_ref[...] * total
        residual_f = ext_ref[e].astype(jnp.float32)
        det = (residual_f - fit).astype(jnp.bfloat16)
        if keep is not None:
            det = (det.astype(jnp.float32) * keep).astype(jnp.bfloat16)
        rows_ref[k] = jnp.dot(blur_ref[...], det, preferred_element_type=jnp.float32)
        return side, fit

    keep_top = edge_ref[0]
    keep_bot = edge_ref[1]

    def top_d(k, side):
        side, _ = detrend(k, side, keep_top)
        return side

    def own_d(r, side):
        side, fit = detrend(GR + r, side, None)
        back_ref[r] = fit.astype(back_ref.dtype)
        return side

    def bot_d(r, side):
        side, _ = detrend(GR + own + r, side, keep_bot)
        return side

    side = lax.fori_loop(0, GR, top_d, side)
    side = lax.fori_loop(0, own, own_d, side)
    side = lax.fori_loop(0, GR, bot_d, side)

    def smooth(y, c):
        acc = taps[GR] * rows_ref[y + GR]
        for o in range(GR):
            acc = acc + taps[o] * (rows_ref[y + o] + rows_ref[y + 2 * GR - o])
        norm_ref[y] = (acc * recip_ref[y]).astype(jnp.bfloat16)
        return c

    lax.fori_loop(0, own, smooth, 0)
    cols, frame_block = norm_ref.shape[1], norm_ref.shape[2]
    grad_ref[...] = jnp.dot(
        frows_ref[...], norm_ref[...].reshape(own * cols, frame_block),
        preferred_element_type=jnp.float32,
    )


def stencil(edge, top, own, bot, scale, recip, frows, frame_block=128):
    halo, own_rows, cols, frames = top.shape[0], own.shape[0], own.shape[1], own.shape[2]
    slots = frows.shape[0]
    ext = 2 * halo + own_rows
    pair, slide, side, blur = band_constants(cols)
    grid = (frames // frame_block,)
    row_block = lambda n: pl.BlockSpec((n, cols, frame_block), lambda j: (0, 0, j))
    fixed = lambda shape: pl.BlockSpec(shape, lambda j: (0,) * len(shape))
    return pl.pallas_call(
        stencil_kernel,
        grid=grid,
        in_specs=[
            pl.BlockSpec(memory_space=pltpu.SMEM),
            row_block(halo), row_block(own_rows), row_block(halo),
            fixed((cols, 2 * cols)), fixed((cols, 2 * cols)), fixed((cols, cols)),
            fixed((cols, cols)), fixed((cols, frame_block)),
            fixed((own_rows, cols, frame_block)), fixed((slots, own_rows * cols)),
        ],
        out_specs=[row_block(own_rows), pl.BlockSpec((slots, frame_block), lambda j: (0, j))],
        out_shape=[jax.ShapeDtypeStruct(own.shape, jnp.bfloat16),
                   jax.ShapeDtypeStruct((slots, frames), jnp.float32)],
        scratch_shapes=[
            pltpu.VMEM((ext, cols, frame_block), jnp.bfloat16),
            pltpu.VMEM((own_rows + 2 * GR, cols, frame_block), jnp.float32),
            pltpu.VMEM((own_rows, cols, frame_block), jnp.bfloat16),
        ],
        compiler_params=pltpu.CompilerParams(vmem_limit_bytes=60 * 1024 * 1024),
    )(edge, top, own, bot, *(jnp.asarray(m) for m in (pair, slide, side, blur)), scale, recip, frows)


MESH = pl.DeviceIdType.MESH


def exchange_kernel(out_ref, in_ref, send_sem, recv_sem, local_sem):
    count = out_ref.shape[0]
    me = lax.axis_index("pix")
    barrier = pltpu.get_barrier_semaphore()

    def peer_at(k):
        return lax.rem(me + k, count)

    def source_at(k):
        return lax.rem(me + count - k, count)

    def remote(target, block):
        return pltpu.make_async_remote_copy(
            src_ref=out_ref.at[target],
            dst_ref=in_ref.at[block],
            send_sem=send_sem.at[target],
            recv_sem=recv_sem.at[block],
            device_id={"pix": target},
            device_id_type=MESH,
        )

    def greet(k, c):
        pl.semaphore_signal(barrier, inc=1, device_id={"pix": peer_at(k)}, device_id_type=MESH)
        return c

    lax.fori_loop(1, count, greet, 0)
    pl.semaphore_wait(barrier, count - 1)

    def launch(k, c):
        remote(peer_at(k), me).start()
        return c

    lax.fori_loop(1, count, launch, 0)
    local = pltpu.make_async_copy(out_ref.at[me], in_ref.at[me], local_sem)
    local.start()
    local.wait()

    def finish(k, c):
        remote(peer_at(k), me).wait_send()
        remote(source_at(k), source_at(k)).wait_recv()
        return c

    lax.fori_loop(1, count, finish, 0)


def exchange(outbox, collective):
    count = outbox.shape[0]
    return pl.pallas_call(
        exchange_kernel,
        out_shape=jax.ShapeDtypeStruct(outbox.shape, outbox.dtype),
        in_specs=[pl.BlockSpec(memory_space=pl.ANY)],
        out_specs=pl.BlockSpec(memory_space=pl.ANY),
        scratch_shapes=[
            pltpu.SemaphoreType.DMA((count,)),
            pltpu.SemaphoreType.DMA((count,)),
            pltpu.SemaphoreType.DMA,
        ],
        compiler_params=pltpu.CompilerParams(collective_id=collective, has_side_effects=True),
    )(outbox)


def on_device(movie, footprints, traces, stripe, column, annulus_gain, decay_slow, decay_fast):
    pix_count = lax.axis_size("pix")
    row_count = movie.shape[1]
    col_count = movie.shape[2]
    frame_count = movie.shape[3]
    neuron_count = footprints.shape[1]
    capacity = max(2, 2 * neuron_count // pix_count)
    slot_count = pix_count * capacity
    target_stripe = stripe[0, :, 0]
    neuron_index = jnp.arange(neuron_count)
    earlier_same = (target_stripe[:, None] == target_stripe[None, :]) & (
        neuron_index[None, :] < neuron_index[:, None]
    )
    arrival_rank = jnp.sum(earlier_same.astype(jnp.int32), axis=1)
    slot_index = target_stripe * capacity + arrival_rank
    placement = slot_index[:, None] == jnp.arange(slot_count)[None, :]
    placement_b = placement.astype(jnp.bfloat16)
    contract_first = (((0,), (0,)), ((), ()))
    tile_width, trace_width = footprints.shape[2], traces.shape[2]
    column_lanes = jnp.broadcast_to(
        (column[0] + 1).astype(jnp.bfloat16)[:, None], (neuron_count, 128)
    )
    payload = jnp.concatenate([footprints[0], traces[0], column_lanes], axis=1)
    outbox = lax.dot_general(
        placement_b, payload, contract_first, preferred_element_type=jnp.float32
    ).astype(jnp.bfloat16)
    inbox = exchange(outbox.reshape(pix_count, capacity, -1), 0).reshape(slot_count, -1)
    tile_inbox = inbox[:, :tile_width]
    trace_inbox = inbox[:, tile_width : tile_width + trace_width]
    column_inbox = inbox[:, tile_width + trace_width].astype(jnp.int32)
    left_edge = column_inbox - 1
    covered = left_edge[:, None] + jnp.arange(FOOT)[None, :]
    column_onehot = (covered[:, :, None] == jnp.arange(col_count)[None, None, :]).astype(
        jnp.bfloat16
    )
    tile_grid = tile_inbox.reshape(slot_count, FOOT, FOOT)
    frows = jnp.einsum(
        "srj,sjc->src", tile_grid, column_onehot, preferred_element_type=jnp.float32
    ).astype(jnp.bfloat16)
    frows_t = jnp.einsum(
        "srj,sjc->rcs", tile_grid, column_onehot, preferred_element_type=jnp.float32
    ).astype(jnp.bfloat16)
    model_image = jnp.einsum(
        "rcs,st->rct", frows_t, trace_inbox, preferred_element_type=jnp.float32
    )
    residual = (movie[0].astype(jnp.float32) - model_image).astype(jnp.bfloat16)
    halo = RAD + GR
    pix_index = lax.axis_index("pix")
    up = [(i, i + 1) for i in range(pix_count - 1)]
    down = [(j, i) for i, j in up]
    top_halo = lax.ppermute(residual[row_count - halo :], "pix", up)
    bottom_halo = lax.ppermute(residual[:halo], "pix", down)
    frame_index = np.arange(frame_count)
    step_matrix = (
        (frame_index[:, None] == frame_index[None, :] + 1).astype(np.float32)
        - (frame_index[:, None] == frame_index[None, :]).astype(np.float32)
    ) * (frame_index[None, :] < frame_count - 1)
    frame_step = jnp.dot(
        residual.reshape(row_count * col_count, frame_count),
        jnp.asarray(step_matrix, jnp.bfloat16),
        preferred_element_type=jnp.float32,
    )
    noise_level = (jnp.sum(frame_step * frame_step, axis=1) / (frame_count - 1)).reshape(
        row_count, col_count
    )
    noise_stack = with_halo(noise_level[None], (("plane", 0),), 1)
    pooled = (noise_stack[0] + 2.0 * noise_stack[1] + noise_stack[2]) / 4.0
    frame_block = 128
    recip = jnp.broadcast_to(
        (1.0 / jnp.sqrt(pooled + noise_eps))[:, :, None], (row_count, col_count, frame_block)
    )
    scale = jnp.broadcast_to((annulus_gain[0] / (8.0 * RAD))[:, None], (col_count, frame_block))
    edge = jnp.stack([pix_index > 0, pix_index < pix_count - 1]).astype(jnp.float32)
    background, slot_gradient = stencil(
        edge, top_halo, residual, bottom_halo, scale, recip,
        frows.reshape(slot_count, row_count * col_count), frame_block
    )
    home_gradient = exchange(slot_gradient.reshape(pix_count, capacity, -1), 1).reshape(
        slot_count, -1
    )
    gradient = lax.dot_general(
        placement.astype(jnp.float32),
        home_gradient,
        (((1,), (0,)), ((), ())),
        precision=lax.Precision.HIGHEST,
    )
    foot_f = footprints[0].astype(jnp.float32)
    step_size = 1.0 / (jnp.sum(foot_f * foot_f, axis=1) + norm_eps)
    updated = traces[0].astype(jnp.float32) + step_size[:, None] * gradient
    spikes = deconvolve(updated, decay_slow[0], decay_fast[0])
    traces_new = reconvolve(spikes, decay_slow[0], decay_fast[0])
    return (background[None], traces_new[None])


def solution(mesh):
    placed = (
        P("plane", "pix", None, None),
        P("plane", "pix", None),
        P("plane", "pix", None),
        P("plane", "pix", None),
        P("plane", "pix"),
        P("plane", None),
        P("plane", "pix"),
        P("plane", "pix"),
    )
    return jax.shard_map(
        on_device,
        mesh=mesh,
        in_specs=placed,
        out_specs=(P("plane", "pix", None, None), P("plane", "pix", None)),
        check_vma=False,
    )
```

```python
import functools
import numpy as np
import ml_dtypes
import jax
import jax.numpy as jnp
from jax import lax
from jax.experimental import pallas as pl
from jax.experimental.pallas import tpu as pltpu
from jax.sharding import PartitionSpec as P

FOOT = 32
RAD = 12
GR = 3


lam_floor = 0.1
noise_eps = 1e-05
norm_eps = 1e-05
sigma_twice = 4.5


def with_halo(array, sides, width):
    for axis, dim in sides:
        devices, length = (lax.axis_size(axis), array.shape[dim])
        up = [(i, (i + 1) % devices) for i in range(devices - 1)]
        down = [(j, i) for i, j in up]
        last = lax.slice_in_dim(array, length - width, length, axis=dim)
        initial = lax.slice_in_dim(array, 0, width, axis=dim)
        before = lax.ppermute(last, axis, up)
        after = lax.ppermute(initial, axis, down)
        array = jnp.concatenate([before, array, after], axis=dim)
    return array


def deconvolve(updated, decay_slow, decay_fast):
    lag_one = jnp.pad(updated, ((0, 0), (1, 0)))[:, :-1]
    lag_two = jnp.pad(updated, ((0, 0), (2, 0)))[:, :-2]
    driven = (
        updated
        - (decay_slow + decay_fast)[:, None] * lag_one
        + (decay_slow * decay_fast)[:, None] * lag_two
    )
    return jnp.maximum(driven - lam_floor, 0.0)


def reconvolve(spikes, decay_slow, decay_fast):
    frame_count = spikes.shape[1]
    slow_col, fast_col = decay_slow[:, None], decay_fast[:, None]

    def geometric_run(values, ratio):
        total, power, shift = values, ratio, 1
        while shift < frame_count:
            lagged = jnp.pad(total, ((0, 0), (shift, 0)))[:, :-shift]
            total = total + power * lagged
            power = power * power
            shift *= 2
        return total

    slow_run = geometric_run(spikes, slow_col)
    fast_run = geometric_run(spikes, fast_col)
    kernel_scale = (1.0 - decay_slow) * (1.0 - decay_fast) / (decay_slow - decay_fast)
    return kernel_scale[:, None] * (slow_col * slow_run - fast_col * fast_run)


def tap_values():
    offsets = np.arange(-GR, GR + 1).astype(np.float64)
    raw = np.exp(-offsets * offsets / sigma_twice)
    taps = (raw / raw.sum()).astype(np.float32).astype(ml_dtypes.bfloat16)
    return taps.astype(np.float32)


def band_constants(col_count):
    index = np.arange(col_count)
    gap = index[None, :] - index[:, None]
    box = (np.abs(gap) <= RAD).astype(np.float32)
    side = (np.abs(gap) == RAD).astype(np.float32)
    taps = tap_values()
    blur = np.zeros((col_count, col_count), np.float32)
    for offset in range(-GR, GR + 1):
        blur = blur + np.where(gap == offset, taps[offset + GR], 0.0)
    as_bf16 = lambda x: x.astype(ml_dtypes.bfloat16)
    pair = np.concatenate([box, box], axis=1)
    slide = np.concatenate([side, -side], axis=1)
    return as_bf16(pair), as_bf16(slide), as_bf16(side), as_bf16(blur)


def stencil_kernel(edge_ref, top_ref, own_ref, bot_ref, pair_ref, slide_ref, side_ref, blur_ref,
                   scale_ref, recip_ref, frows_hbm, back_ref, grad_ref, ext_ref, rows_ref, norm_ref,
                   frows_ref, frows_sem):
    halo = top_ref.shape[0]
    own = own_ref.shape[0]
    taps = [float(v) for v in tap_values()]
    first_step = pl.program_id(0) == 0
    frows_copy = pltpu.make_async_copy(frows_hbm, frows_ref, frows_sem)

    @pl.when(first_step)
    def _():
        frows_copy.start()

    def copy_top(r, c):
        ext_ref[r] = top_ref[r]
        return c

    def copy_own(r, c):
        ext_ref[halo + r] = own_ref[r]
        return c

    def copy_bot(r, c):
        ext_ref[halo + own + r] = bot_ref[r]
        return c

    lax.fori_loop(0, halo, copy_top, 0)
    lax.fori_loop(0, own, copy_own, 0)
    lax.fori_loop(0, halo, copy_bot, 0)

    first = halo - GR
    side = jnp.dot(side_ref[...], ext_ref[first - RAD], preferred_element_type=jnp.float32)
    for i in range(1, 2 * RAD - 1):
        side = side + jnp.dot(
            side_ref[...], ext_ref[first - RAD + i], preferred_element_type=jnp.float32
        )

    def detrend(k, side, keep):
        e = first + k
        above, below = ext_ref[e - RAD], ext_ref[e + RAD]
        step = jnp.dot(
            slide_ref[...], jnp.concatenate([ext_ref[e + RAD - 1], above], axis=0),
            preferred_element_type=jnp.float32,
        )
        side = side + step
        ring = jnp.dot(
            pair_ref[...], jnp.concatenate([above, below], axis=0),
            preferred_element_type=jnp.float32,
        )
        total = ring + side
        fit = scale_ref[...] * total
        residual_f = ext_ref[e].astype(jnp.float32)
        det = (residual_f - fit).astype(jnp.bfloat16)
        if keep is not None:
            det = (det.astype(jnp.float32) * keep).astype(jnp.bfloat16)
        rows_ref[k] = jnp.dot(blur_ref[...], det, preferred_element_type=jnp.float32)
        return side, fit

    keep_top = edge_ref[0]
    keep_bot = edge_ref[1]

    def top_d(k, side):
        side, _ = detrend(k, side, keep_top)
        return side

    def own_d(r, side):
        side, fit = detrend(GR + r, side, None)
        back_ref[r] = fit.astype(back_ref.dtype)
        return side

    def bot_d(r, side):
        side, _ = detrend(GR + own + r, side, keep_bot)
        return side

    side = lax.fori_loop(0, GR, top_d, side)
    side = lax.fori_loop(0, own, own_d, side)
    side = lax.fori_loop(0, GR, bot_d, side)

    def smooth(y, c):
        acc = taps[GR] * rows_ref[y + GR]
        for o in range(GR):
            acc = acc + taps[o] * (rows_ref[y + o] + rows_ref[y + 2 * GR - o])
        norm_ref[y] = (acc * recip_ref[y]).astype(jnp.bfloat16)
        return c

    lax.fori_loop(0, own, smooth, 0)
    cols, frame_block = norm_ref.shape[1], norm_ref.shape[2]

    @pl.when(first_step)
    def _():
        frows_copy.wait()

    grad_ref[...] = jnp.dot(
        frows_ref[...], norm_ref[...].reshape(own * cols, frame_block),
        preferred_element_type=jnp.float32,
    )


def stencil(edge, top, own, bot, scale, recip, frows, frame_block=128):
    halo, own_rows, cols, frames = top.shape[0], own.shape[0], own.shape[1], own.shape[2]
    slots = frows.shape[0]
    ext = 2 * halo + own_rows
    pair, slide, side, blur = band_constants(cols)
    grid = (frames // frame_block,)
    row_block = lambda n: pl.BlockSpec((n, cols, frame_block), lambda j: (0, 0, j))
    fixed = lambda shape: pl.BlockSpec(shape, lambda j: (0,) * len(shape))
    return pl.pallas_call(
        stencil_kernel,
        grid=grid,
        in_specs=[
            pl.BlockSpec(memory_space=pltpu.SMEM),
            row_block(halo), row_block(own_rows), row_block(halo),
            fixed((cols, 2 * cols)), fixed((cols, 2 * cols)), fixed((cols, cols)),
            fixed((cols, cols)), fixed((cols, frame_block)),
            fixed((own_rows, cols, frame_block)), pl.BlockSpec(memory_space=pl.ANY),
        ],
        out_specs=[row_block(own_rows), pl.BlockSpec((slots, frame_block), lambda j: (0, j))],
        out_shape=[jax.ShapeDtypeStruct(own.shape, jnp.bfloat16),
                   jax.ShapeDtypeStruct((slots, frames), jnp.float32)],
        scratch_shapes=[
            pltpu.VMEM((ext, cols, frame_block), jnp.bfloat16),
            pltpu.VMEM((own_rows + 2 * GR, cols, frame_block), jnp.float32),
            pltpu.VMEM((own_rows, cols, frame_block), jnp.bfloat16),
            pltpu.VMEM((slots, own_rows * cols), jnp.bfloat16),
            pltpu.SemaphoreType.DMA,
        ],
        compiler_params=pltpu.CompilerParams(vmem_limit_bytes=60 * 1024 * 1024),
    )(edge, top, own, bot, *(jnp.asarray(m) for m in (pair, slide, side, blur)), scale, recip, frows)


MESH = pl.DeviceIdType.MESH


def exchange_kernel(out_ref, in_ref, send_sem, recv_sem, local_sem):
    count = out_ref.shape[0]
    me = lax.axis_index("pix")
    barrier = pltpu.get_barrier_semaphore()

    def peer_at(k):
        return lax.rem(me + k, count)

    def source_at(k):
        return lax.rem(me + count - k, count)

    def remote(target, block):
        return pltpu.make_async_remote_copy(
            src_ref=out_ref.at[target],
            dst_ref=in_ref.at[block],
            send_sem=send_sem.at[target],
            recv_sem=recv_sem.at[block],
            device_id={"pix": target},
            device_id_type=MESH,
        )

    def greet(k, c):
        pl.semaphore_signal(barrier, inc=1, device_id={"pix": peer_at(k)}, device_id_type=MESH)
        return c

    lax.fori_loop(1, count, greet, 0)
    pl.semaphore_wait(barrier, count - 1)

    def launch(k, c):
        remote(peer_at(k), me).start()
        return c

    lax.fori_loop(1, count, launch, 0)
    local = pltpu.make_async_copy(out_ref.at[me], in_ref.at[me], local_sem)
    local.start()
    local.wait()

    def finish(k, c):
        remote(peer_at(k), me).wait_send()
        remote(source_at(k), source_at(k)).wait_recv()
        return c

    lax.fori_loop(1, count, finish, 0)


def exchange(outbox, collective):
    count = outbox.shape[0]
    return pl.pallas_call(
        exchange_kernel,
        out_shape=jax.ShapeDtypeStruct(outbox.shape, outbox.dtype),
        in_specs=[pl.BlockSpec(memory_space=pl.ANY)],
        out_specs=pl.BlockSpec(memory_space=pl.ANY),
        scratch_shapes=[
            pltpu.SemaphoreType.DMA((count,)),
            pltpu.SemaphoreType.DMA((count,)),
            pltpu.SemaphoreType.DMA,
        ],
        compiler_params=pltpu.CompilerParams(collective_id=collective, has_side_effects=True),
    )(outbox)


def on_device(movie, footprints, traces, stripe, column, annulus_gain, decay_slow, decay_fast):
    pix_count = lax.axis_size("pix")
    row_count = movie.shape[1]
    col_count = movie.shape[2]
    frame_count = movie.shape[3]
    neuron_count = footprints.shape[1]
    capacity = max(2, 2 * neuron_count // pix_count)
    slot_count = pix_count * capacity
    target_stripe = stripe[0, :, 0]
    neuron_index = jnp.arange(neuron_count)
    earlier_same = (target_stripe[:, None] == target_stripe[None, :]) & (
        neuron_index[None, :] < neuron_index[:, None]
    )
    arrival_rank = jnp.sum(earlier_same.astype(jnp.int32), axis=1)
    slot_index = target_stripe * capacity + arrival_rank
    placement = slot_index[:, None] == jnp.arange(slot_count)[None, :]
    placement_b = placement.astype(jnp.bfloat16)
    contract_first = (((0,), (0,)), ((), ()))
    tile_width, trace_width = footprints.shape[2], traces.shape[2]
    column_lanes = jnp.broadcast_to(
        (column[0] + 1).astype(jnp.bfloat16)[:, None], (neuron_count, 128)
    )
    payload = jnp.concatenate([footprints[0], traces[0], column_lanes], axis=1)
    outbox = lax.dot_general(
        placement_b, payload, contract_first, preferred_element_type=jnp.float32
    ).astype(jnp.bfloat16)
    inbox = exchange(outbox.reshape(pix_count, capacity, -1), 0).reshape(slot_count, -1)
    tile_inbox = inbox[:, :tile_width]
    trace_inbox = inbox[:, tile_width : tile_width + trace_width]
    column_inbox = inbox[:, tile_width + trace_width].astype(jnp.int32)
    left_edge = column_inbox - 1
    covered = left_edge[:, None] + jnp.arange(FOOT)[None, :]
    column_onehot = (covered[:, :, None] == jnp.arange(col_count)[None, None, :]).astype(
        jnp.bfloat16
    )
    tile_grid = tile_inbox.reshape(slot_count, FOOT, FOOT)
    frows = jnp.einsum(
        "srj,sjc->src", tile_grid, column_onehot, preferred_element_type=jnp.float32
    ).astype(jnp.bfloat16)
    frows_t = jnp.einsum(
        "srj,sjc->rcs", tile_grid, column_onehot, preferred_element_type=jnp.float32
    ).astype(jnp.bfloat16)
    model_image = jnp.einsum(
        "rcs,st->rct", frows_t, trace_inbox, preferred_element_type=jnp.float32
    )
    residual = (movie[0].astype(jnp.float32) - model_image).astype(jnp.bfloat16)
    halo = RAD + GR
    pix_index = lax.axis_index("pix")
    up = [(i, i + 1) for i in range(pix_count - 1)]
    down = [(j, i) for i, j in up]
    top_halo = lax.ppermute(residual[row_count - halo :], "pix", up)
    bottom_halo = lax.ppermute(residual[:halo], "pix", down)
    frame_index = np.arange(frame_count)
    step_matrix = (
        (frame_index[:, None] == frame_index[None, :] + 1).astype(np.float32)
        - (frame_index[:, None] == frame_index[None, :]).astype(np.float32)
    ) * (frame_index[None, :] < frame_count - 1)
    frame_step = jnp.dot(
        residual.reshape(row_count * col_count, frame_count),
        jnp.asarray(step_matrix, jnp.bfloat16),
        preferred_element_type=jnp.float32,
    )
    noise_level = (jnp.sum(frame_step * frame_step, axis=1) / (frame_count - 1)).reshape(
        row_count, col_count
    )
    noise_stack = with_halo(noise_level[None], (("plane", 0),), 1)
    pooled = (noise_stack[0] + 2.0 * noise_stack[1] + noise_stack[2]) / 4.0
    frame_block = 128
    recip = jnp.broadcast_to(
        (1.0 / jnp.sqrt(pooled + noise_eps))[:, :, None], (row_count, col_count, frame_block)
    )
    scale = jnp.broadcast_to((annulus_gain[0] / (8.0 * RAD))[:, None], (col_count, frame_block))
    edge = jnp.stack([pix_index > 0, pix_index < pix_count - 1]).astype(jnp.float32)
    background, slot_gradient = stencil(
        edge, top_halo, residual, bottom_halo, scale, recip,
        frows.reshape(slot_count, row_count * col_count), frame_block
    )
    home_gradient = exchange(slot_gradient.reshape(pix_count, capacity, -1), 1).reshape(
        slot_count, -1
    )
    gradient = lax.dot_general(
        placement.astype(jnp.float32),
        home_gradient,
        (((1,), (0,)), ((), ())),
        precision=lax.Precision.HIGHEST,
    )
    foot_f = footprints[0].astype(jnp.float32)
    step_size = 1.0 / (jnp.sum(foot_f * foot_f, axis=1) + norm_eps)
    updated = traces[0].astype(jnp.float32) + step_size[:, None] * gradient
    spikes = deconvolve(updated, decay_slow[0], decay_fast[0])
    traces_new = reconvolve(spikes, decay_slow[0], decay_fast[0])
    return (background[None], traces_new[None])


def solution(mesh):
    placed = (
        P("plane", "pix", None, None),
        P("plane", "pix", None),
        P("plane", "pix", None),
        P("plane", "pix", None),
        P("plane", "pix"),
        P("plane", None),
        P("plane", "pix"),
        P("plane", "pix"),
    )
    return jax.shard_map(
        on_device,
        mesh=mesh,
        in_specs=placed,
        out_specs=(P("plane", "pix", None, None), P("plane", "pix", None)),
        check_vma=False,
    )
```

```python
import functools
import numpy as np
import ml_dtypes
import jax
import jax.numpy as jnp
from jax import lax
from jax.experimental import pallas as pl
from jax.experimental.pallas import tpu as pltpu
from jax.sharding import PartitionSpec as P

FOOT = 32
RAD = 12
GR = 3


lam_floor = 0.1
noise_eps = 1e-05
norm_eps = 1e-05
sigma_twice = 4.5


def with_halo(array, sides, width):
    for axis, dim in sides:
        devices, length = (lax.axis_size(axis), array.shape[dim])
        up = [(i, (i + 1) % devices) for i in range(devices - 1)]
        down = [(j, i) for i, j in up]
        last = lax.slice_in_dim(array, length - width, length, axis=dim)
        initial = lax.slice_in_dim(array, 0, width, axis=dim)
        before = lax.ppermute(last, axis, up)
        after = lax.ppermute(initial, axis, down)
        array = jnp.concatenate([before, array, after], axis=dim)
    return array


def deconvolve(updated, decay_slow, decay_fast):
    lag_one = jnp.pad(updated, ((0, 0), (1, 0)))[:, :-1]
    lag_two = jnp.pad(updated, ((0, 0), (2, 0)))[:, :-2]
    driven = (
        updated
        - (decay_slow + decay_fast)[:, None] * lag_one
        + (decay_slow * decay_fast)[:, None] * lag_two
    )
    return jnp.maximum(driven - lam_floor, 0.0)


def reconvolve(spikes, decay_slow, decay_fast):
    frame_count = spikes.shape[1]
    slow_col, fast_col = decay_slow[:, None], decay_fast[:, None]

    def geometric_run(values, ratio):
        total, power, shift = values, ratio, 1
        while shift < frame_count:
            lagged = jnp.pad(total, ((0, 0), (shift, 0)))[:, :-shift]
            total = total + power * lagged
            power = power * power
            shift *= 2
        return total

    slow_run = geometric_run(spikes, slow_col)
    fast_run = geometric_run(spikes, fast_col)
    kernel_scale = (1.0 - decay_slow) * (1.0 - decay_fast) / (decay_slow - decay_fast)
    return kernel_scale[:, None] * (slow_col * slow_run - fast_col * fast_run)


def tap_values():
    offsets = np.arange(-GR, GR + 1).astype(np.float64)
    raw = np.exp(-offsets * offsets / sigma_twice)
    taps = (raw / raw.sum()).astype(np.float32).astype(ml_dtypes.bfloat16)
    return taps.astype(np.float32)


def band_constants(col_count):
    index = np.arange(col_count)
    gap = index[None, :] - index[:, None]
    box = (np.abs(gap) <= RAD).astype(np.float32)
    side = (np.abs(gap) == RAD).astype(np.float32)
    taps = tap_values()
    blur = np.zeros((col_count, col_count), np.float32)
    for offset in range(-GR, GR + 1):
        blur = blur + np.where(gap == offset, taps[offset + GR], 0.0)
    as_bf16 = lambda x: x.astype(ml_dtypes.bfloat16)
    pair = np.concatenate([box, box], axis=1)
    slide = np.concatenate([side, -side], axis=1)
    return as_bf16(pair), as_bf16(slide), as_bf16(side), as_bf16(blur)


def stencil_kernel(edge_ref, top_ref, own_ref, bot_ref, pair_ref, slide_ref, side_ref, blur_ref,
                   scale_ref, recip_hbm, frows_hbm, back_ref, grad_ref, ext_ref, rows_ref, norm_ref,
                   frows_ref, frows_sem, recip_ref, recip_sem):
    halo = top_ref.shape[0]
    own = own_ref.shape[0]
    taps = [float(v) for v in tap_values()]
    first_step = pl.program_id(0) == 0
    frows_copy = pltpu.make_async_copy(frows_hbm, frows_ref, frows_sem)
    recip_copy = pltpu.make_async_copy(recip_hbm, recip_ref, recip_sem)

    @pl.when(first_step)
    def _():
        recip_copy.start()
        frows_copy.start()

    def copy_top(r, c):
        ext_ref[r] = top_ref[r]
        return c

    def copy_own(r, c):
        ext_ref[halo + r] = own_ref[r]
        return c

    def copy_bot(r, c):
        ext_ref[halo + own + r] = bot_ref[r]
        return c

    lax.fori_loop(0, halo, copy_top, 0)
    lax.fori_loop(0, own, copy_own, 0)
    lax.fori_loop(0, halo, copy_bot, 0)

    first = halo - GR
    side = jnp.dot(side_ref[...], ext_ref[first - RAD], preferred_element_type=jnp.float32)
    for i in range(1, 2 * RAD - 1):
        side = side + jnp.dot(
            side_ref[...], ext_ref[first - RAD + i], preferred_element_type=jnp.float32
        )

    def detrend(k, side, keep):
        e = first + k
        above, below = ext_ref[e - RAD], ext_ref[e + RAD]
        step = jnp.dot(
            slide_ref[...], jnp.concatenate([ext_ref[e + RAD - 1], above], axis=0),
            preferred_element_type=jnp.float32,
        )
        side = side + step
        ring = jnp.dot(
            pair_ref[...], jnp.concatenate([above, below], axis=0),
            preferred_element_type=jnp.float32,
        )
        total = ring + side
        fit = scale_ref[...] * total
        residual_f = ext_ref[e].astype(jnp.float32)
        det = (residual_f - fit).astype(jnp.bfloat16)
        if keep is not None:
            det = (det.astype(jnp.float32) * keep).astype(jnp.bfloat16)
        rows_ref[k] = jnp.dot(blur_ref[...], det, preferred_element_type=jnp.float32)
        return side, fit

    keep_top = edge_ref[0]
    keep_bot = edge_ref[1]

    def top_d(k, side):
        side, _ = detrend(k, side, keep_top)
        return side

    def own_d(r, side):
        side, fit = detrend(GR + r, side, None)
        back_ref[r] = fit.astype(back_ref.dtype)
        return side

    def bot_d(r, side):
        side, _ = detrend(GR + own + r, side, keep_bot)
        return side

    side = lax.fori_loop(0, GR, top_d, side)
    side = lax.fori_loop(0, own, own_d, side)
    side = lax.fori_loop(0, GR, bot_d, side)

    @pl.when(first_step)
    def _():
        recip_copy.wait()

    def smooth(y, c):
        acc = taps[GR] * rows_ref[y + GR]
        for o in range(GR):
            acc = acc + taps[o] * (rows_ref[y + o] + rows_ref[y + 2 * GR - o])
        norm_ref[y] = (acc * recip_ref[y]).astype(jnp.bfloat16)
        return c

    lax.fori_loop(0, own, smooth, 0)
    cols, frame_block = norm_ref.shape[1], norm_ref.shape[2]

    @pl.when(first_step)
    def _():
        frows_copy.wait()

    grad_ref[...] = jnp.dot(
        frows_ref[...], norm_ref[...].reshape(own * cols, frame_block),
        preferred_element_type=jnp.float32,
    )


def stencil(edge, top, own, bot, scale, recip, frows, frame_block=128):
    halo, own_rows, cols, frames = top.shape[0], own.shape[0], own.shape[1], own.shape[2]
    slots = frows.shape[0]
    ext = 2 * halo + own_rows
    pair, slide, side, blur = band_constants(cols)
    grid = (frames // frame_block,)
    row_block = lambda n: pl.BlockSpec((n, cols, frame_block), lambda j: (0, 0, j))
    fixed = lambda shape: pl.BlockSpec(shape, lambda j: (0,) * len(shape))
    return pl.pallas_call(
        stencil_kernel,
        grid=grid,
        in_specs=[
            pl.BlockSpec(memory_space=pltpu.SMEM),
            row_block(halo), row_block(own_rows), row_block(halo),
            fixed((cols, 2 * cols)), fixed((cols, 2 * cols)), fixed((cols, cols)),
            fixed((cols, cols)), fixed((cols, frame_block)),
            pl.BlockSpec(memory_space=pl.ANY), pl.BlockSpec(memory_space=pl.ANY),
        ],
        out_specs=[row_block(own_rows), pl.BlockSpec((slots, frame_block), lambda j: (0, j))],
        out_shape=[jax.ShapeDtypeStruct(own.shape, jnp.bfloat16),
                   jax.ShapeDtypeStruct((slots, frames), jnp.float32)],
        scratch_shapes=[
            pltpu.VMEM((ext, cols, frame_block), jnp.bfloat16),
            pltpu.VMEM((own_rows + 2 * GR, cols, frame_block), jnp.float32),
            pltpu.VMEM((own_rows, cols, frame_block), jnp.bfloat16),
            pltpu.VMEM((slots, own_rows * cols), jnp.bfloat16),
            pltpu.SemaphoreType.DMA,
            pltpu.VMEM((own_rows, cols, frame_block), jnp.float32),
            pltpu.SemaphoreType.DMA,
        ],
        compiler_params=pltpu.CompilerParams(vmem_limit_bytes=60 * 1024 * 1024),
    )(edge, top, own, bot, *(jnp.asarray(m) for m in (pair, slide, side, blur)), scale, recip, frows)


MESH = pl.DeviceIdType.MESH


def exchange_kernel(out_ref, in_ref, send_sem, recv_sem, local_sem):
    count = out_ref.shape[0]
    me = lax.axis_index("pix")
    barrier = pltpu.get_barrier_semaphore()

    def peer_at(k):
        return lax.rem(me + k, count)

    def source_at(k):
        return lax.rem(me + count - k, count)

    def remote(target, block):
        return pltpu.make_async_remote_copy(
            src_ref=out_ref.at[target],
            dst_ref=in_ref.at[block],
            send_sem=send_sem.at[target],
            recv_sem=recv_sem.at[block],
            device_id={"pix": target},
            device_id_type=MESH,
        )

    def greet(k, c):
        pl.semaphore_signal(barrier, inc=1, device_id={"pix": peer_at(k)}, device_id_type=MESH)
        return c

    lax.fori_loop(1, count, greet, 0)
    pl.semaphore_wait(barrier, count - 1)

    def launch(k, c):
        remote(peer_at(k), me).start()
        return c

    lax.fori_loop(1, count, launch, 0)
    local = pltpu.make_async_copy(out_ref.at[me], in_ref.at[me], local_sem)
    local.start()
    local.wait()

    def finish(k, c):
        remote(peer_at(k), me).wait_send()
        remote(source_at(k), source_at(k)).wait_recv()
        return c

    lax.fori_loop(1, count, finish, 0)


def exchange(outbox, collective):
    count = outbox.shape[0]
    return pl.pallas_call(
        exchange_kernel,
        out_shape=jax.ShapeDtypeStruct(outbox.shape, outbox.dtype),
        in_specs=[pl.BlockSpec(memory_space=pl.ANY)],
        out_specs=pl.BlockSpec(memory_space=pl.ANY),
        scratch_shapes=[
            pltpu.SemaphoreType.DMA((count,)),
            pltpu.SemaphoreType.DMA((count,)),
            pltpu.SemaphoreType.DMA,
        ],
        compiler_params=pltpu.CompilerParams(collective_id=collective, has_side_effects=True),
    )(outbox)


def on_device(movie, footprints, traces, stripe, column, annulus_gain, decay_slow, decay_fast):
    pix_count = lax.axis_size("pix")
    row_count = movie.shape[1]
    col_count = movie.shape[2]
    frame_count = movie.shape[3]
    neuron_count = footprints.shape[1]
    capacity = max(2, 2 * neuron_count // pix_count)
    slot_count = pix_count * capacity
    target_stripe = stripe[0, :, 0]
    neuron_index = jnp.arange(neuron_count)
    earlier_same = (target_stripe[:, None] == target_stripe[None, :]) & (
        neuron_index[None, :] < neuron_index[:, None]
    )
    arrival_rank = jnp.sum(earlier_same.astype(jnp.int32), axis=1)
    slot_index = target_stripe * capacity + arrival_rank
    placement = slot_index[:, None] == jnp.arange(slot_count)[None, :]
    placement_b = placement.astype(jnp.bfloat16)
    contract_first = (((0,), (0,)), ((), ()))
    tile_width, trace_width = footprints.shape[2], traces.shape[2]
    column_lanes = jnp.broadcast_to(
        (column[0] + 1).astype(jnp.bfloat16)[:, None], (neuron_count, 128)
    )
    payload = jnp.concatenate([footprints[0], traces[0], column_lanes], axis=1)
    placement_3d = placement_b.reshape(neuron_count, pix_count, capacity)
    outbox = jnp.einsum(
        "ndk,nw->dkw", placement_3d, payload, preferred_element_type=jnp.float32
    ).astype(jnp.bfloat16)
    inbox = exchange(outbox, 0).reshape(slot_count, -1)
    tile_inbox = inbox[:, :tile_width]
    trace_inbox = inbox[:, tile_width : tile_width + trace_width]
    column_inbox = inbox[:, tile_width + trace_width].astype(jnp.int32)
    left_edge = column_inbox - 1
    covered = left_edge[:, None] + jnp.arange(FOOT)[None, :]
    column_onehot = (covered[:, :, None] == jnp.arange(col_count)[None, None, :]).astype(
        jnp.bfloat16
    )
    tile_grid = tile_inbox.reshape(slot_count, FOOT, FOOT)
    frows = jnp.einsum(
        "srj,sjc->src", tile_grid, column_onehot, preferred_element_type=jnp.float32
    ).astype(jnp.bfloat16)
    frows_t = jnp.einsum(
        "srj,sjc->rcs", tile_grid, column_onehot, preferred_element_type=jnp.float32
    ).astype(jnp.bfloat16)
    model_image = jnp.einsum(
        "rcs,st->rct", frows_t, trace_inbox, preferred_element_type=jnp.float32
    )
    residual = (movie[0].astype(jnp.float32) - model_image).astype(jnp.bfloat16)
    halo = RAD + GR
    pix_index = lax.axis_index("pix")
    up = [(i, i + 1) for i in range(pix_count - 1)]
    down = [(j, i) for i, j in up]
    top_halo = lax.ppermute(residual[row_count - halo :], "pix", up)
    bottom_halo = lax.ppermute(residual[:halo], "pix", down)
    frame_index = np.arange(frame_count)
    step_matrix = (
        (frame_index[:, None] == frame_index[None, :] + 1).astype(np.float32)
        - (frame_index[:, None] == frame_index[None, :]).astype(np.float32)
    ) * (frame_index[None, :] < frame_count - 1)
    frame_step = jnp.dot(
        residual.reshape(row_count * col_count, frame_count),
        jnp.asarray(step_matrix, jnp.bfloat16),
        preferred_element_type=jnp.float32,
    )
    noise_level = (jnp.sum(frame_step * frame_step, axis=1) / (frame_count - 1)).reshape(
        row_count, col_count
    )
    noise_stack = with_halo(noise_level[None], (("plane", 0),), 1)
    pooled = (noise_stack[0] + 2.0 * noise_stack[1] + noise_stack[2]) / 4.0
    frame_block = 128
    recip = jnp.broadcast_to(
        (1.0 / jnp.sqrt(pooled + noise_eps))[:, :, None], (row_count, col_count, frame_block)
    )
    scale = jnp.broadcast_to((annulus_gain[0] / (8.0 * RAD))[:, None], (col_count, frame_block))
    edge = jnp.stack([pix_index > 0, pix_index < pix_count - 1]).astype(jnp.float32)
    background, slot_gradient = stencil(
        edge, top_halo, residual, bottom_halo, scale, recip,
        frows.reshape(slot_count, row_count * col_count), frame_block
    )
    home_gradient = exchange(slot_gradient.reshape(pix_count, capacity, -1), 1)
    gradient = jnp.einsum(
        "ndk,dkf->nf",
        placement.astype(jnp.float32).reshape(neuron_count, pix_count, capacity),
        home_gradient,
        precision=lax.Precision.HIGHEST,
    )
    foot_f = footprints[0].astype(jnp.float32)
    step_size = 1.0 / (jnp.sum(foot_f * foot_f, axis=1) + norm_eps)
    updated = traces[0].astype(jnp.float32) + step_size[:, None] * gradient
    spikes = deconvolve(updated, decay_slow[0], decay_fast[0])
    traces_new = reconvolve(spikes, decay_slow[0], decay_fast[0])
    return (background[None], traces_new[None])


def solution(mesh):
    placed = (
        P("plane", "pix", None, None),
        P("plane", "pix", None),
        P("plane", "pix", None),
        P("plane", "pix", None),
        P("plane", "pix"),
        P("plane", None),
        P("plane", "pix"),
        P("plane", "pix"),
    )
    return jax.shard_map(
        on_device,
        mesh=mesh,
        in_specs=placed,
        out_specs=(P("plane", "pix", None, None), P("plane", "pix", None)),
        check_vma=False,
    )
```

```python
import functools
import numpy as np
import ml_dtypes
import jax
import jax.numpy as jnp
from jax import lax
from jax.experimental import pallas as pl
from jax.experimental.pallas import tpu as pltpu
from jax.sharding import PartitionSpec as P

FOOT = 32
RAD = 12
GR = 3


lam_floor = 0.1
noise_eps = 1e-05
norm_eps = 1e-05
sigma_twice = 4.5


def with_halo(array, sides, width):
    for axis, dim in sides:
        devices, length = (lax.axis_size(axis), array.shape[dim])
        up = [(i, (i + 1) % devices) for i in range(devices - 1)]
        down = [(j, i) for i, j in up]
        last = lax.slice_in_dim(array, length - width, length, axis=dim)
        initial = lax.slice_in_dim(array, 0, width, axis=dim)
        before = lax.ppermute(last, axis, up)
        after = lax.ppermute(initial, axis, down)
        array = jnp.concatenate([before, array, after], axis=dim)
    return array


def deconvolve(updated, decay_slow, decay_fast):
    lag_one = jnp.pad(updated, ((0, 0), (1, 0)))[:, :-1]
    lag_two = jnp.pad(updated, ((0, 0), (2, 0)))[:, :-2]
    driven = (
        updated
        - (decay_slow + decay_fast)[:, None] * lag_one
        + (decay_slow * decay_fast)[:, None] * lag_two
    )
    return jnp.maximum(driven - lam_floor, 0.0)


def reconvolve(spikes, decay_slow, decay_fast):
    frame_count = spikes.shape[1]
    slow_col, fast_col = decay_slow[:, None], decay_fast[:, None]

    def geometric_run(values, ratio):
        total, power, shift = values, ratio, 1
        while shift < frame_count:
            lagged = jnp.pad(total, ((0, 0), (shift, 0)))[:, :-shift]
            total = total + power * lagged
            power = power * power
            shift *= 2
        return total

    slow_run = geometric_run(spikes, slow_col)
    fast_run = geometric_run(spikes, fast_col)
    kernel_scale = (1.0 - decay_slow) * (1.0 - decay_fast) / (decay_slow - decay_fast)
    return kernel_scale[:, None] * (slow_col * slow_run - fast_col * fast_run)


def tap_values():
    offsets = np.arange(-GR, GR + 1).astype(np.float64)
    raw = np.exp(-offsets * offsets / sigma_twice)
    taps = (raw / raw.sum()).astype(np.float32).astype(ml_dtypes.bfloat16)
    return taps.astype(np.float32)


def band_constants(col_count):
    index = np.arange(col_count)
    gap = index[None, :] - index[:, None]
    box = (np.abs(gap) <= RAD).astype(np.float32)
    side = (np.abs(gap) == RAD).astype(np.float32)
    taps = tap_values()
    blur = np.zeros((col_count, col_count), np.float32)
    for offset in range(-GR, GR + 1):
        blur = blur + np.where(gap == offset, taps[offset + GR], 0.0)
    as_bf16 = lambda x: x.astype(ml_dtypes.bfloat16)
    pair = np.concatenate([box, box], axis=1)
    slide = np.concatenate([side, -side], axis=1)
    return as_bf16(pair), as_bf16(slide), as_bf16(side), as_bf16(blur)


def stencil_kernel(edge_ref, top_ref, own_ref, bot_ref, pair_ref, slide_ref, side_ref, blur_ref,
                   scale_ref, recip_hbm, frows_hbm, back_ref, grad_ref, ext_ref, rows_ref, norm_ref,
                   frows_ref, frows_sem, recip_ref, recip_sem):
    halo = top_ref.shape[0]
    own = own_ref.shape[0]
    taps = [float(v) for v in tap_values()]
    first_step = pl.program_id(0) == 0
    frows_copy = pltpu.make_async_copy(frows_hbm, frows_ref, frows_sem)
    recip_copy = pltpu.make_async_copy(recip_hbm, recip_ref, recip_sem)

    @pl.when(first_step)
    def _():
        recip_copy.start()
        frows_copy.start()

    def copy_top(r, c):
        ext_ref[r] = top_ref[r]
        return c

    def copy_own(r, c):
        ext_ref[halo + r] = own_ref[r]
        return c

    def copy_bot(r, c):
        ext_ref[halo + own + r] = bot_ref[r]
        return c

    lax.fori_loop(0, halo, copy_top, 0)
    lax.fori_loop(0, own, copy_own, 0)
    lax.fori_loop(0, halo, copy_bot, 0)

    first = halo - GR
    column_sum = ext_ref[first - RAD].astype(jnp.float32)
    for i in range(1, 2 * RAD - 1):
        column_sum = column_sum + ext_ref[first - RAD + i].astype(jnp.float32)
    high = column_sum.astype(jnp.bfloat16)
    rest = column_sum - high.astype(jnp.float32)
    middle = rest.astype(jnp.bfloat16)
    low = (rest - middle.astype(jnp.float32)).astype(jnp.bfloat16)
    side = jnp.dot(side_ref[...], high, preferred_element_type=jnp.float32)
    side = side + jnp.dot(side_ref[...], middle, preferred_element_type=jnp.float32)
    side = side + jnp.dot(side_ref[...], low, preferred_element_type=jnp.float32)

    def detrend(k, side, keep):
        e = first + k
        above, below = ext_ref[e - RAD], ext_ref[e + RAD]
        step = jnp.dot(
            slide_ref[...], jnp.concatenate([ext_ref[e + RAD - 1], above], axis=0),
            preferred_element_type=jnp.float32,
        )
        side = side + step
        ring = jnp.dot(
            pair_ref[...], jnp.concatenate([above, below], axis=0),
            preferred_element_type=jnp.float32,
        )
        total = ring + side
        fit = scale_ref[...] * total
        residual_f = ext_ref[e].astype(jnp.float32)
        det = (residual_f - fit).astype(jnp.bfloat16)
        if keep is not None:
            det = (det.astype(jnp.float32) * keep).astype(jnp.bfloat16)
        rows_ref[k] = jnp.dot(blur_ref[...], det, preferred_element_type=jnp.float32)
        return side, fit

    keep_top = edge_ref[0]
    keep_bot = edge_ref[1]

    def top_d(k, side):
        side, _ = detrend(k, side, keep_top)
        return side

    def own_d(r, side):
        side, fit = detrend(GR + r, side, None)
        back_ref[r] = fit.astype(back_ref.dtype)
        return side

    def bot_d(r, side):
        side, _ = detrend(GR + own + r, side, keep_bot)
        return side

    side = lax.fori_loop(0, GR, top_d, side)
    side = lax.fori_loop(0, own, own_d, side)
    side = lax.fori_loop(0, GR, bot_d, side)

    @pl.when(first_step)
    def _():
        recip_copy.wait()

    def smooth(y, c):
        acc = taps[GR] * rows_ref[y + GR]
        for o in range(GR):
            acc = acc + taps[o] * (rows_ref[y + o] + rows_ref[y + 2 * GR - o])
        norm_ref[y] = (acc * recip_ref[y]).astype(jnp.bfloat16)
        return c

    lax.fori_loop(0, own, smooth, 0)
    cols, frame_block = norm_ref.shape[1], norm_ref.shape[2]

    @pl.when(first_step)
    def _():
        frows_copy.wait()

    grad_ref[...] = jnp.dot(
        frows_ref[...], norm_ref[...].reshape(own * cols, frame_block),
        preferred_element_type=jnp.float32,
    )


def stencil(edge, top, own, bot, scale, recip, frows, frame_block=128):
    halo, own_rows, cols, frames = top.shape[0], own.shape[0], own.shape[1], own.shape[2]
    slots = frows.shape[0]
    ext = 2 * halo + own_rows
    pair, slide, side, blur = band_constants(cols)
    grid = (frames // frame_block,)
    row_block = lambda n: pl.BlockSpec((n, cols, frame_block), lambda j: (0, 0, j))
    fixed = lambda shape: pl.BlockSpec(shape, lambda j: (0,) * len(shape))
    return pl.pallas_call(
        stencil_kernel,
        grid=grid,
        in_specs=[
            pl.BlockSpec(memory_space=pltpu.SMEM),
            row_block(halo), row_block(own_rows), row_block(halo),
            fixed((cols, 2 * cols)), fixed((cols, 2 * cols)), fixed((cols, cols)),
            fixed((cols, cols)), fixed((cols, frame_block)),
            pl.BlockSpec(memory_space=pl.ANY), pl.BlockSpec(memory_space=pl.ANY),
        ],
        out_specs=[row_block(own_rows), pl.BlockSpec((slots, frame_block), lambda j: (0, j))],
        out_shape=[jax.ShapeDtypeStruct(own.shape, jnp.bfloat16),
                   jax.ShapeDtypeStruct((slots, frames), jnp.float32)],
        scratch_shapes=[
            pltpu.VMEM((ext, cols, frame_block), jnp.bfloat16),
            pltpu.VMEM((own_rows + 2 * GR, cols, frame_block), jnp.float32),
            pltpu.VMEM((own_rows, cols, frame_block), jnp.bfloat16),
            pltpu.VMEM((slots, own_rows * cols), jnp.bfloat16),
            pltpu.SemaphoreType.DMA,
            pltpu.VMEM((own_rows, cols, frame_block), jnp.float32),
            pltpu.SemaphoreType.DMA,
        ],
        compiler_params=pltpu.CompilerParams(vmem_limit_bytes=60 * 1024 * 1024),
    )(edge, top, own, bot, *(jnp.asarray(m) for m in (pair, slide, side, blur)), scale, recip, frows)


MESH = pl.DeviceIdType.MESH


def exchange_kernel(out_ref, in_ref, send_sem, recv_sem, local_sem):
    count = out_ref.shape[0]
    me = lax.axis_index("pix")
    barrier = pltpu.get_barrier_semaphore()

    def peer_at(k):
        return lax.rem(me + k, count)

    def source_at(k):
        return lax.rem(me + count - k, count)

    def remote(target, block):
        return pltpu.make_async_remote_copy(
            src_ref=out_ref.at[target],
            dst_ref=in_ref.at[block],
            send_sem=send_sem.at[target],
            recv_sem=recv_sem.at[block],
            device_id={"pix": target},
            device_id_type=MESH,
        )

    def greet(k, c):
        pl.semaphore_signal(barrier, inc=1, device_id={"pix": peer_at(k)}, device_id_type=MESH)
        return c

    lax.fori_loop(1, count, greet, 0)
    pl.semaphore_wait(barrier, count - 1)

    def launch(k, c):
        remote(peer_at(k), me).start()
        return c

    lax.fori_loop(1, count, launch, 0)
    local = pltpu.make_async_copy(out_ref.at[me], in_ref.at[me], local_sem)
    local.start()
    local.wait()

    def finish(k, c):
        remote(peer_at(k), me).wait_send()
        remote(source_at(k), source_at(k)).wait_recv()
        return c

    lax.fori_loop(1, count, finish, 0)


def exchange(outbox, collective):
    count = outbox.shape[0]
    return pl.pallas_call(
        exchange_kernel,
        out_shape=jax.ShapeDtypeStruct(outbox.shape, outbox.dtype),
        in_specs=[pl.BlockSpec(memory_space=pl.ANY)],
        out_specs=pl.BlockSpec(memory_space=pl.ANY),
        scratch_shapes=[
            pltpu.SemaphoreType.DMA((count,)),
            pltpu.SemaphoreType.DMA((count,)),
            pltpu.SemaphoreType.DMA,
        ],
        compiler_params=pltpu.CompilerParams(collective_id=collective, has_side_effects=True),
    )(outbox)


def on_device(movie, footprints, traces, stripe, column, annulus_gain, decay_slow, decay_fast):
    pix_count = lax.axis_size("pix")
    row_count = movie.shape[1]
    col_count = movie.shape[2]
    frame_count = movie.shape[3]
    neuron_count = footprints.shape[1]
    capacity = max(2, 2 * neuron_count // pix_count)
    slot_count = pix_count * capacity
    target_stripe = stripe[0, :, 0]
    neuron_index = jnp.arange(neuron_count)
    earlier_same = (target_stripe[:, None] == target_stripe[None, :]) & (
        neuron_index[None, :] < neuron_index[:, None]
    )
    arrival_rank = jnp.sum(earlier_same.astype(jnp.int32), axis=1)
    slot_index = target_stripe * capacity + arrival_rank
    placement = slot_index[:, None] == jnp.arange(slot_count)[None, :]
    placement_b = placement.astype(jnp.bfloat16)
    contract_first = (((0,), (0,)), ((), ()))
    tile_width, trace_width = footprints.shape[2], traces.shape[2]
    column_lanes = jnp.broadcast_to(
        (column[0] + 1).astype(jnp.bfloat16)[:, None], (neuron_count, 128)
    )
    payload = jnp.concatenate([footprints[0], traces[0], column_lanes], axis=1)
    placement_3d = placement_b.reshape(neuron_count, pix_count, capacity)
    outbox = jnp.einsum(
        "ndk,nw->dkw", placement_3d, payload, preferred_element_type=jnp.float32
    ).astype(jnp.bfloat16)
    inbox = exchange(outbox, 0).reshape(slot_count, -1)
    tile_inbox = inbox[:, :tile_width]
    trace_inbox = inbox[:, tile_width : tile_width + trace_width]
    column_inbox = inbox[:, tile_width + trace_width].astype(jnp.int32)
    left_edge = column_inbox - 1
    covered = left_edge[:, None] + jnp.arange(FOOT)[None, :]
    column_onehot = (covered[:, :, None] == jnp.arange(col_count)[None, None, :]).astype(
        jnp.bfloat16
    )
    tile_grid = tile_inbox.reshape(slot_count, FOOT, FOOT)
    frows = jnp.einsum(
        "srj,sjc->src", tile_grid, column_onehot, preferred_element_type=jnp.float32
    ).astype(jnp.bfloat16)
    frows_t = jnp.einsum(
        "srj,sjc->rcs", tile_grid, column_onehot, preferred_element_type=jnp.float32
    ).astype(jnp.bfloat16)
    model_image = jnp.einsum(
        "rcs,st->rct", frows_t, trace_inbox, preferred_element_type=jnp.float32
    )
    residual = (movie[0].astype(jnp.float32) - model_image).astype(jnp.bfloat16)
    halo = RAD + GR
    pix_index = lax.axis_index("pix")
    up = [(i, i + 1) for i in range(pix_count - 1)]
    down = [(j, i) for i, j in up]
    top_halo = lax.ppermute(residual[row_count - halo :], "pix", up)
    bottom_halo = lax.ppermute(residual[:halo], "pix", down)
    frame_index = np.arange(frame_count)
    step_matrix = (
        (frame_index[:, None] == frame_index[None, :] + 1).astype(np.float32)
        - (frame_index[:, None] == frame_index[None, :]).astype(np.float32)
    ) * (frame_index[None, :] < frame_count - 1)
    frame_step = jnp.dot(
        residual.reshape(row_count * col_count, frame_count),
        jnp.asarray(step_matrix, jnp.bfloat16),
        preferred_element_type=jnp.float32,
    )
    noise_level = (jnp.sum(frame_step * frame_step, axis=1) / (frame_count - 1)).reshape(
        row_count, col_count
    )
    noise_stack = with_halo(noise_level[None], (("plane", 0),), 1)
    pooled = (noise_stack[0] + 2.0 * noise_stack[1] + noise_stack[2]) / 4.0
    frame_block = 128
    recip = jnp.broadcast_to(
        (1.0 / jnp.sqrt(pooled + noise_eps))[:, :, None], (row_count, col_count, frame_block)
    )
    scale = jnp.broadcast_to((annulus_gain[0] / (8.0 * RAD))[:, None], (col_count, frame_block))
    edge = jnp.stack([pix_index > 0, pix_index < pix_count - 1]).astype(jnp.float32)
    background, slot_gradient = stencil(
        edge, top_halo, residual, bottom_halo, scale, recip,
        frows.reshape(slot_count, row_count * col_count), frame_block
    )
    home_gradient = exchange(slot_gradient.reshape(pix_count, capacity, -1), 1)
    gradient = jnp.einsum(
        "ndk,dkf->nf",
        placement.astype(jnp.float32).reshape(neuron_count, pix_count, capacity),
        home_gradient,
        precision=lax.Precision.HIGHEST,
    )
    foot_f = footprints[0].astype(jnp.float32)
    step_size = 1.0 / (jnp.sum(foot_f * foot_f, axis=1) + norm_eps)
    updated = traces[0].astype(jnp.float32) + step_size[:, None] * gradient
    spikes = deconvolve(updated, decay_slow[0], decay_fast[0])
    traces_new = reconvolve(spikes, decay_slow[0], decay_fast[0])
    return (background[None], traces_new[None])


def solution(mesh):
    placed = (
        P("plane", "pix", None, None),
        P("plane", "pix", None),
        P("plane", "pix", None),
        P("plane", "pix", None),
        P("plane", "pix"),
        P("plane", None),
        P("plane", "pix"),
        P("plane", "pix"),
    )
    return jax.shard_map(
        on_device,
        mesh=mesh,
        in_specs=placed,
        out_specs=(P("plane", "pix", None, None), P("plane", "pix", None)),
        check_vma=False,
    )
```

```python
import functools
import numpy as np
import ml_dtypes
import jax
import jax.numpy as jnp
from jax import lax
from jax.experimental import pallas as pl
from jax.experimental.pallas import tpu as pltpu
from jax.sharding import PartitionSpec as P

FOOT = 32
RAD = 12
GR = 3


lam_floor = 0.1
noise_eps = 1e-05
norm_eps = 1e-05
sigma_twice = 4.5


def with_halo(array, sides, width):
    for axis, dim in sides:
        devices, length = (lax.axis_size(axis), array.shape[dim])
        up = [(i, (i + 1) % devices) for i in range(devices - 1)]
        down = [(j, i) for i, j in up]
        last = lax.slice_in_dim(array, length - width, length, axis=dim)
        initial = lax.slice_in_dim(array, 0, width, axis=dim)
        before = lax.ppermute(last, axis, up)
        after = lax.ppermute(initial, axis, down)
        array = jnp.concatenate([before, array, after], axis=dim)
    return array


def deconvolve(updated, decay_slow, decay_fast):
    lag_one = jnp.pad(updated, ((0, 0), (1, 0)))[:, :-1]
    lag_two = jnp.pad(updated, ((0, 0), (2, 0)))[:, :-2]
    driven = (
        updated
        - (decay_slow + decay_fast)[:, None] * lag_one
        + (decay_slow * decay_fast)[:, None] * lag_two
    )
    return jnp.maximum(driven - lam_floor, 0.0)


def reconvolve(spikes, decay_slow, decay_fast):
    frame_count = spikes.shape[1]
    slow_col, fast_col = decay_slow[:, None], decay_fast[:, None]

    def geometric_run(values, ratio):
        total, power, shift = values, ratio, 1
        while shift < frame_count:
            lagged = jnp.pad(total, ((0, 0), (shift, 0)))[:, :-shift]
            total = total + power * lagged
            power = power * power
            shift *= 2
        return total

    slow_run = geometric_run(spikes, slow_col)
    fast_run = geometric_run(spikes, fast_col)
    kernel_scale = (1.0 - decay_slow) * (1.0 - decay_fast) / (decay_slow - decay_fast)
    return kernel_scale[:, None] * (slow_col * slow_run - fast_col * fast_run)


def tap_values():
    offsets = np.arange(-GR, GR + 1).astype(np.float64)
    raw = np.exp(-offsets * offsets / sigma_twice)
    taps = (raw / raw.sum()).astype(np.float32).astype(ml_dtypes.bfloat16)
    return taps.astype(np.float32)


def band_constants(col_count):
    index = np.arange(col_count)
    gap = index[None, :] - index[:, None]
    box = (np.abs(gap) <= RAD).astype(np.float32)
    side = (np.abs(gap) == RAD).astype(np.float32)
    taps = tap_values()
    blur = np.zeros((col_count, col_count), np.float32)
    for offset in range(-GR, GR + 1):
        blur = blur + np.where(gap == offset, taps[offset + GR], 0.0)
    as_bf16 = lambda x: x.astype(ml_dtypes.bfloat16)
    pair = np.concatenate([box, box], axis=1)
    slide = np.concatenate([side, -side], axis=1)
    return as_bf16(pair), as_bf16(slide), as_bf16(side), as_bf16(blur)


def stencil_kernel(edge_ref, top_ref, own_ref, bot_ref, pair_ref, slide_ref, side_ref, blur_ref,
                   scale_ref, recip_hbm, frows_hbm, back_ref, grad_ref, ext_ref, rows_ref, norm_ref,
                   frows_ref, frows_sem, recip_ref, recip_sem):
    halo = top_ref.shape[0]
    own = own_ref.shape[0]
    taps = [float(v) for v in tap_values()]
    first_step = pl.program_id(0) == 0
    frows_copy = pltpu.make_async_copy(frows_hbm, frows_ref, frows_sem)
    recip_copy = pltpu.make_async_copy(recip_hbm, recip_ref, recip_sem)

    @pl.when(first_step)
    def _():
        recip_copy.start()
        frows_copy.start()

    def copy_top(r, c):
        ext_ref[r] = top_ref[r]
        return c

    def copy_own(r, c):
        ext_ref[halo + r] = own_ref[r]
        return c

    def copy_bot(r, c):
        ext_ref[halo + own + r] = bot_ref[r]
        return c

    lax.fori_loop(0, halo, copy_top, 0)
    lax.fori_loop(0, own, copy_own, 0)
    lax.fori_loop(0, halo, copy_bot, 0)

    first = halo - GR
    column_sum = ext_ref[first - RAD].astype(jnp.float32)
    for i in range(1, 2 * RAD - 1):
        column_sum = column_sum + ext_ref[first - RAD + i].astype(jnp.float32)
    high = column_sum.astype(jnp.bfloat16)
    rest = column_sum - high.astype(jnp.float32)
    middle = rest.astype(jnp.bfloat16)
    low = (rest - middle.astype(jnp.float32)).astype(jnp.bfloat16)
    side = jnp.dot(side_ref[...], high, preferred_element_type=jnp.float32)
    side = side + jnp.dot(side_ref[...], middle, preferred_element_type=jnp.float32)
    side = side + jnp.dot(side_ref[...], low, preferred_element_type=jnp.float32)

    def detrend(k, side, keep):
        e = first + k
        above, below = ext_ref[e - RAD], ext_ref[e + RAD]
        step = jnp.dot(
            slide_ref[...], jnp.concatenate([ext_ref[e + RAD - 1], above], axis=0),
            preferred_element_type=jnp.float32,
        )
        side = side + step
        ring = jnp.dot(
            pair_ref[...], jnp.concatenate([above, below], axis=0),
            preferred_element_type=jnp.float32,
        )
        total = ring + side
        fit = scale_ref[...] * total
        residual_f = ext_ref[e].astype(jnp.float32)
        det = (residual_f - fit).astype(jnp.bfloat16)
        if keep is not None:
            det = (det.astype(jnp.float32) * keep).astype(jnp.bfloat16)
        rows_ref[k] = jnp.dot(blur_ref[...], det, preferred_element_type=jnp.float32)
        return side, fit

    keep_top = edge_ref[0]
    keep_bot = edge_ref[1]

    def top_d(k, side):
        side, _ = detrend(k, side, keep_top)
        return side

    def own_d(r, side):
        side, fit = detrend(GR + r, side, None)
        back_ref[r] = fit.astype(back_ref.dtype)
        return side

    def bot_d(r, side):
        side, _ = detrend(GR + own + r, side, keep_bot)
        return side

    side = lax.fori_loop(0, GR, top_d, side)
    side = lax.fori_loop(0, own, own_d, side)
    side = lax.fori_loop(0, GR, bot_d, side)

    @pl.when(first_step)
    def _():
        recip_copy.wait()

    def smooth(y, c):
        acc = taps[GR] * rows_ref[y + GR]
        for o in range(GR):
            acc = acc + taps[o] * (rows_ref[y + o] + rows_ref[y + 2 * GR - o])
        norm_ref[y] = (acc * recip_ref[y]).astype(jnp.bfloat16)
        return c

    lax.fori_loop(0, own, smooth, 0)
    cols, frame_block = norm_ref.shape[1], norm_ref.shape[2]

    @pl.when(first_step)
    def _():
        frows_copy.wait()

    grad_ref[...] = jnp.dot(
        frows_ref[...], norm_ref[...].reshape(own * cols, frame_block),
        preferred_element_type=jnp.float32,
    )


def stencil(edge, top, own, bot, scale, recip, frows, frame_block=128):
    halo, own_rows, cols, frames = top.shape[0], own.shape[0], own.shape[1], own.shape[2]
    slots = frows.shape[0]
    ext = 2 * halo + own_rows
    pair, slide, side, blur = band_constants(cols)
    grid = (frames // frame_block,)
    row_block = lambda n: pl.BlockSpec((n, cols, frame_block), lambda j: (0, 0, j))
    fixed = lambda shape: pl.BlockSpec(shape, lambda j: (0,) * len(shape))
    return pl.pallas_call(
        stencil_kernel,
        grid=grid,
        in_specs=[
            pl.BlockSpec(memory_space=pltpu.SMEM),
            row_block(halo), row_block(own_rows), row_block(halo),
            fixed((cols, 2 * cols)), fixed((cols, 2 * cols)), fixed((cols, cols)),
            fixed((cols, cols)), fixed((cols, frame_block)),
            pl.BlockSpec(memory_space=pl.ANY), pl.BlockSpec(memory_space=pl.ANY),
        ],
        out_specs=[row_block(own_rows), pl.BlockSpec((slots, frame_block), lambda j: (0, j))],
        out_shape=[jax.ShapeDtypeStruct(own.shape, jnp.bfloat16),
                   jax.ShapeDtypeStruct((slots, frames), jnp.float32)],
        scratch_shapes=[
            pltpu.VMEM((ext, cols, frame_block), jnp.bfloat16),
            pltpu.VMEM((own_rows + 2 * GR, cols, frame_block), jnp.float32),
            pltpu.VMEM((own_rows, cols, frame_block), jnp.bfloat16),
            pltpu.VMEM((slots, own_rows * cols), jnp.bfloat16),
            pltpu.SemaphoreType.DMA,
            pltpu.VMEM((own_rows, cols, frame_block), jnp.float32),
            pltpu.SemaphoreType.DMA,
        ],
        compiler_params=pltpu.CompilerParams(vmem_limit_bytes=60 * 1024 * 1024),
    )(edge, top, own, bot, *(jnp.asarray(m) for m in (pair, slide, side, blur)), scale, recip, frows)


MESH = pl.DeviceIdType.MESH


def exchange_kernel(out_ref, in_ref, send_sem, recv_sem, local_sem):
    count = out_ref.shape[0]
    me = lax.axis_index("pix")
    barrier = pltpu.get_barrier_semaphore()

    def peer_at(k):
        return lax.rem(me + k, count)

    def source_at(k):
        return lax.rem(me + count - k, count)

    def remote(target, block):
        return pltpu.make_async_remote_copy(
            src_ref=out_ref.at[target],
            dst_ref=in_ref.at[block],
            send_sem=send_sem.at[target],
            recv_sem=recv_sem.at[block],
            device_id={"pix": target},
            device_id_type=MESH,
        )

    def greet(k, c):
        pl.semaphore_signal(barrier, inc=1, device_id={"pix": peer_at(k)}, device_id_type=MESH)
        return c

    lax.fori_loop(1, count, greet, 0)
    local = pltpu.make_async_copy(out_ref.at[me], in_ref.at[me], local_sem)
    local.start()
    pl.semaphore_wait(barrier, count - 1)

    def launch(k, c):
        remote(peer_at(k), me).start()
        return c

    lax.fori_loop(1, count, launch, 0)
    local.wait()

    def finish(k, c):
        remote(peer_at(k), me).wait_send()
        remote(source_at(k), source_at(k)).wait_recv()
        return c

    lax.fori_loop(1, count, finish, 0)


def exchange(outbox, collective):
    count = outbox.shape[0]
    return pl.pallas_call(
        exchange_kernel,
        out_shape=jax.ShapeDtypeStruct(outbox.shape, outbox.dtype),
        in_specs=[pl.BlockSpec(memory_space=pl.ANY)],
        out_specs=pl.BlockSpec(memory_space=pl.ANY),
        scratch_shapes=[
            pltpu.SemaphoreType.DMA((count,)),
            pltpu.SemaphoreType.DMA((count,)),
            pltpu.SemaphoreType.DMA,
        ],
        compiler_params=pltpu.CompilerParams(collective_id=collective, has_side_effects=True),
    )(outbox)


def on_device(movie, footprints, traces, stripe, column, annulus_gain, decay_slow, decay_fast):
    pix_count = lax.axis_size("pix")
    row_count = movie.shape[1]
    col_count = movie.shape[2]
    frame_count = movie.shape[3]
    neuron_count = footprints.shape[1]
    capacity = max(2, 2 * neuron_count // pix_count)
    slot_count = pix_count * capacity
    target_stripe = stripe[0, :, 0]
    neuron_index = jnp.arange(neuron_count)
    earlier_same = (target_stripe[:, None] == target_stripe[None, :]) & (
        neuron_index[None, :] < neuron_index[:, None]
    )
    arrival_rank = jnp.sum(earlier_same.astype(jnp.int32), axis=1)
    slot_index = target_stripe * capacity + arrival_rank
    placement = slot_index[:, None] == jnp.arange(slot_count)[None, :]
    placement_b = placement.astype(jnp.bfloat16)
    contract_first = (((0,), (0,)), ((), ()))
    tile_width, trace_width = footprints.shape[2], traces.shape[2]
    column_lanes = jnp.broadcast_to(
        (column[0] + 1).astype(jnp.bfloat16)[:, None], (neuron_count, 128)
    )
    payload = jnp.concatenate([footprints[0], traces[0], column_lanes], axis=1)
    placement_3d = placement_b.reshape(neuron_count, pix_count, capacity)
    outbox = jnp.einsum(
        "ndk,nw->dkw", placement_3d, payload, preferred_element_type=jnp.float32
    ).astype(jnp.bfloat16)
    inbox = exchange(outbox, 0).reshape(slot_count, -1)
    tile_inbox = inbox[:, :tile_width]
    trace_inbox = inbox[:, tile_width : tile_width + trace_width]
    column_inbox = inbox[:, tile_width + trace_width].astype(jnp.int32)
    left_edge = column_inbox - 1
    covered = left_edge[:, None] + jnp.arange(FOOT)[None, :]
    column_onehot = (covered[:, :, None] == jnp.arange(col_count)[None, None, :]).astype(
        jnp.bfloat16
    )
    tile_grid = tile_inbox.reshape(slot_count, FOOT, FOOT)
    frows = jnp.einsum(
        "srj,sjc->src", tile_grid, column_onehot, preferred_element_type=jnp.float32
    ).astype(jnp.bfloat16)
    frows_t = jnp.einsum(
        "srj,sjc->rcs", tile_grid, column_onehot, preferred_element_type=jnp.float32
    ).astype(jnp.bfloat16)
    model_image = jnp.einsum(
        "rcs,st->rct", frows_t, trace_inbox, preferred_element_type=jnp.float32
    )
    residual = (movie[0].astype(jnp.float32) - model_image).astype(jnp.bfloat16)
    halo = RAD + GR
    pix_index = lax.axis_index("pix")
    up = [(i, i + 1) for i in range(pix_count - 1)]
    down = [(j, i) for i, j in up]
    top_halo = lax.ppermute(residual[row_count - halo :], "pix", up)
    bottom_halo = lax.ppermute(residual[:halo], "pix", down)
    frame_index = np.arange(frame_count)
    step_matrix = (
        (frame_index[:, None] == frame_index[None, :] + 1).astype(np.float32)
        - (frame_index[:, None] == frame_index[None, :]).astype(np.float32)
    ) * (frame_index[None, :] < frame_count - 1)
    frame_step = jnp.dot(
        residual.reshape(row_count * col_count, frame_count),
        jnp.asarray(step_matrix, jnp.bfloat16),
        preferred_element_type=jnp.float32,
    )
    noise_level = (jnp.sum(frame_step * frame_step, axis=1) / (frame_count - 1)).reshape(
        row_count, col_count
    )
    noise_stack = with_halo(noise_level[None], (("plane", 0),), 1)
    pooled = (noise_stack[0] + 2.0 * noise_stack[1] + noise_stack[2]) / 4.0
    frame_block = 128
    recip = jnp.broadcast_to(
        (1.0 / jnp.sqrt(pooled + noise_eps))[:, :, None], (row_count, col_count, frame_block)
    )
    scale = jnp.broadcast_to((annulus_gain[0] / (8.0 * RAD))[:, None], (col_count, frame_block))
    edge = jnp.stack([pix_index > 0, pix_index < pix_count - 1]).astype(jnp.float32)
    background, slot_gradient = stencil(
        edge, top_halo, residual, bottom_halo, scale, recip,
        frows.reshape(slot_count, row_count * col_count), frame_block
    )
    home_gradient = exchange(slot_gradient.reshape(pix_count, capacity, -1), 1)
    gradient = jnp.einsum(
        "ndk,dkf->nf",
        placement.astype(jnp.float32).reshape(neuron_count, pix_count, capacity),
        home_gradient,
        precision=lax.Precision.HIGHEST,
    )
    foot_f = footprints[0].astype(jnp.float32)
    step_size = 1.0 / (jnp.sum(foot_f * foot_f, axis=1) + norm_eps)
    updated = traces[0].astype(jnp.float32) + step_size[:, None] * gradient
    spikes = deconvolve(updated, decay_slow[0], decay_fast[0])
    traces_new = reconvolve(spikes, decay_slow[0], decay_fast[0])
    return (background[None], traces_new[None])


def solution(mesh):
    placed = (
        P("plane", "pix", None, None),
        P("plane", "pix", None),
        P("plane", "pix", None),
        P("plane", "pix", None),
        P("plane", "pix"),
        P("plane", None),
        P("plane", "pix"),
        P("plane", "pix"),
    )
    return jax.shard_map(
        on_device,
        mesh=mesh,
        in_specs=placed,
        out_specs=(P("plane", "pix", None, None), P("plane", "pix", None)),
        check_vma=False,
    )
```
